32 devices in a mesh: mem: 4 (over y, x), gx: 4 (over z), gy: 2 (over core).
Axes of the slice: x: 2, y: 2, z: 4, core: 2. Of those that a mesh axis runs over, the one named last changes fastest.
Arguments:
- control: float32 [2, 16, 512, 512], P(None, 'mem', 'gx', 'gy'), may hold values from -6 to 6
- members: float32 [8, 2, 16, 256, 256], P('mem', None, None, 'gx', 'gy'), may hold values from -6 to 6
- diffusivity: float32 [16, 256, 256], P(None, 'gx', 'gy'), may hold values from 0.05 to 0.4
- rotation: float32 [256, 256], P('gx', 'gy'), may hold values from -1 to 1
Outputs:
- control_final: float32 [2, 16, 512, 512], P(None, 'mem', 'gx', 'gy')
- members_final: float32 [8, 2, 16, 256, 256], P('mem', None, None, 'gx', 'gy')
The draws below stay inside these ranges and needn't reach their ends.
All inputs are finite; a program needn't handle non-finite values.
Results may differ from the reference program's by a relative error of at most 0.00002.
Values sent between devices are 32-bit elements; how exact they have to be, the bound alone decides.
A program may use at most 128 MiB of HBM per device.

```python
import math
import jax
import jax.numpy as jnp
from jax import lax

LEV = 16
CSTEPS = 4
MSTEPS = 4
NX = 512
NY = 512
MX = 256
MY = 256
MEMBERS = 8


def level_of(stream_key, dims, pieces, low, largest):
    factor_of = 1.0
    for axis_at, parts in pieces:
        heights = jax.random.uniform(jax.random.fold_in(jax.random.fold_in(stream_key, 6), axis_at), (parts,), jnp.float32, low / len(pieces), largest / len(pieces))
        factor_of = factor_of * jnp.repeat(jnp.exp(heights), dims[axis_at] // parts).reshape((-1,) + (1,) * (len(dims) - 1 - axis_at))
    return factor_of


def gaussian(stream_key, extent, deviation, bound, pieces=(), dtype=jnp.bfloat16):
    values = jax.random.normal(stream_key, extent, jnp.float32) * deviation
    if len(pieces) > 0:
        values = level_of(stream_key, extent, pieces, -0.22, 0.18) * values
    return jnp.clip(values, min=-bound, max=bound).astype(dtype)


def setup_inputs(seed: int = 0) -> dict:
    streams_of = jax.random.split(jax.random.key(seed), 5)
    control = gaussian(streams_of[0], (2, LEV, NX, NY), 1.0, 6.0, ((1, 4), (2, 4), (3, 2)), jnp.float32)
    members = gaussian(streams_of[1], (MEMBERS, 2, LEV, MX, MY), 1.0, 6.0, ((0, 4), (3, 4), (4, 2)), jnp.float32)
    diffusivity = jnp.clip(jnp.exp(math.log(0.4) - 2.0794415 * jax.random.uniform(streams_of[2], (LEV, MX, MY), jnp.float32) ** level_of(streams_of[2], (LEV, MX, MY), ((1, 4), (2, 2)), -0.2, 0.2)), 0.05, 0.4)
    rotation = jnp.clip(jax.random.uniform(streams_of[3], (MX, MY), jnp.float32, -1.0, 1.0) * level_of(streams_of[3], (MX, MY), ((0, 4), (1, 2)), -0.4, 0.0), -1.0, 1.0)
    return {"control": control, "members": members, "diffusivity": diffusivity, "rotation": rotation}


step_control = 0.15
viscosity = 0.5
step_member = 0.5


def control_step(fields):
    upper_x = jnp.roll(fields, -1, axis=-2)
    lower_x = jnp.roll(fields, 1, axis=-2)
    upper_y = jnp.roll(fields, -1, axis=-1)
    lower_y = jnp.roll(fields, 1, axis=-1)
    along_x = (upper_x - lower_x) * 0.5
    along_y = (upper_y - lower_y) * 0.5
    laplace = upper_x + lower_x + upper_y + lower_y - 4.0 * fields
    speed_x = fields[0:1]
    speed_y = fields[1:2]
    return fields + step_control * (-speed_x * along_x - speed_y * along_y + viscosity * laplace)


def member_step(ensemble, east, west, north, south, rotation):
    upper_x = jnp.roll(ensemble, -1, axis=-2)
    lower_x = jnp.roll(ensemble, 1, axis=-2)
    upper_y = jnp.roll(ensemble, -1, axis=-1)
    lower_y = jnp.roll(ensemble, 1, axis=-1)
    spread = east * (upper_x - ensemble) - west * (ensemble - lower_x) + north * (upper_y - ensemble) - south * (ensemble - lower_y)
    first = ensemble[:, 0]
    second = ensemble[:, 1]
    new_first = first + step_member * (spread[:, 0] - rotation * second)
    new_second = second + step_member * (spread[:, 1] + rotation * first)
    return jnp.stack([new_first, new_second], axis=1)


def reference(control, members, diffusivity, rotation):
    def per_level(inputs):
        fields, ensemble, kappa = inputs
        for repeat in range(CSTEPS):
            fields = control_step(fields)
        restricted = fields.reshape(2, NX // 2, 2, NY // 2, 2).sum(axis=(2, 4)) * 0.25
        mean = jnp.sum(ensemble, axis=0) / MEMBERS
        ensemble = ensemble + (restricted - mean)[None]
        east = 0.5 * (kappa + jnp.roll(kappa, -1, axis=-2))
        west = 0.5 * (jnp.roll(kappa, 1, axis=-2) + kappa)
        north = 0.5 * (kappa + jnp.roll(kappa, -1, axis=-1))
        south = 0.5 * (jnp.roll(kappa, 1, axis=-1) + kappa)
        for repeat in range(MSTEPS):
            ensemble = member_step(ensemble, east, west, north, south, rotation)
        return fields, ensemble

    control_levels = jnp.moveaxis(control, 1, 0)
    member_levels = jnp.moveaxis(members, 2, 0)
    fields_out, ensemble_out = lax.map(per_level, (control_levels, member_levels, diffusivity))
    return jnp.moveaxis(fields_out, 0, 1), jnp.moveaxis(ensemble_out, 0, 2)
```

```python
import functools

import jax
import jax.numpy as jnp
from jax import lax
from jax.experimental import pallas as pl
from jax.experimental.pallas import tpu as pltpu
from jax.sharding import PartitionSpec as P

CSTEPS = 4
MSTEPS = 4
H = 4
SLOT = 2 * H
LANES = 128

step_control = 0.15
viscosity = 0.5
step_member = 0.5
F32 = jnp.float32


def lane_ids(rows):
    return lax.broadcasted_iota(jnp.int32, (rows, LANES), 1)


def put_slot(packed, edges, slot):
    shift = H + SLOT * slot
    if not isinstance(slot, int):
        shift = lax.rem(shift, LANES)
    rolled = pltpu.roll(edges, shift, 1)
    ids = lane_ids(edges.shape[0])
    inside = (ids >= SLOT * slot) & (ids < SLOT * slot + SLOT)
    return jnp.where(inside, rolled, packed)


def side_block(left, right, slot):
    shift = lax.rem(2 * LANES - SLOT * slot - H, LANES)
    after = pltpu.roll(right, shift, 1)
    if left is right:
        return after
    before = pltpu.roll(left, shift, 1)
    return jnp.where(lane_ids(after.shape[0]) < LANES // 2, after, before)


def fused_kernel(
    copies, c_ref, m_ref, d_ref, r_ref, cf_ref, mf_ref,
    hc, tc, nc, prc, hm, tm, nm, prm, yc, ym, yc_in, ym_in, ccor, mcor, ccor_in, mcor_in,
    sums, sums_in, corr, hcorr, tcorr, ncorr, prcorr, ycorr, ycorr_in, kcor, kcor_in,
    shift, shift_in, mx, dx, rx, kx, ih, kih, strips, kstrips, edge_coef, halos, khalo, wtop, wbot,
    send_sem, recv_sem,
):
    fields, clevels, crows, ccols = c_ref.shape
    count, _, levels, rows, cols = m_ref.shape
    base = count * fields
    nx, ny, n = lax.axis_size("gx"), lax.axis_size("gy"), lax.axis_size("mem")
    x, y, me = lax.axis_index("gx"), lax.axis_index("gy"), lax.axis_index("mem")
    two = ny > 2
    nsides = 2 if two else 1
    x_next, x_prev = {"gx": lax.rem(x + 1, nx)}, {"gx": lax.rem(x + nx - 1, nx)}
    y_next, y_prev = {"gy": lax.rem(y + 1, ny)}, {"gy": lax.rem(y + ny - 1, ny)}
    peers = [{"mem": lax.rem(me + k, n)} for k in range(1, n)]
    mesh_id = pl.DeviceIdType.MESH
    pending = []

    def send(src, dst, target):
        k = len(pending)
        copy = pltpu.make_async_remote_copy(
            src_ref=src, dst_ref=dst, send_sem=send_sem.at[k], recv_sem=recv_sem.at[k],
            device_id=target, device_id_type=mesh_id,
        )
        copy.start()
        pending.append(copy)
        return copy

    def landed(group):
        for copy in group:
            copy.wait_recv()

    def send_y(src, dst):
        group = [send(src, dst.at[0], y_next)]
        if two:
            group.append(send(src, dst.at[1], y_prev))
        return group

    def send_x(first, last, from_next, from_prev):
        return [send(first, from_next, x_prev), send(last, from_prev, x_next)]

    def send_corners(got, buf, buf_in):
        group = []
        for side in range(nsides):
            for g in range(got.shape[1]):
                tile = got[side, g]
                buf[side, 0, g] = tile[:H]
                buf[side, 1, g] = tile[tile.shape[0] - H :]
            group += send_x(
                buf.at[side, 0], buf.at[side, 1], buf_in.at[side, 0], buf_in.at[side, 1]
            )
        return group

    barrier = pltpu.get_barrier_semaphore()
    greeted = [x_next, x_prev, y_next] + ([y_prev] if two else []) + peers
    for target in greeted:
        pl.semaphore_signal(barrier, inc=1, device_id=target, device_id_type=mesh_id)

    ids = lane_ids(crows)
    yc[...] = jnp.zeros_like(yc)
    ym[...] = jnp.zeros_like(ym)
    ycorr[...] = jnp.zeros_like(ycorr)

    @pl.loop(0, clevels)
    def _(l):
        for f in range(fields):
            first = c_ref[f, l, :, :LANES]
            last = c_ref[f, l, :, ccols - LANES :]
            t = f * clevels + l
            yc[0] = put_slot(yc[0], jnp.where(ids < LANES // 2, first, last), t)
            hc[t] = c_ref[f, l, :H]
            tc[t] = c_ref[f, l, crows - H :]

    pl.semaphore_wait(barrier, len(greeted))
    got_yc = send_y(yc, yc_in)
    got_xc = send_x(hc, tc, nc, prc)

    @pl.loop(0, levels)
    def _(l):
        for f in range(fields):
            total = None
            for m in range(count):
                tile = m_ref[m, f, l]
                total = tile if total is None else total + tile
                g = m * fields + f
                mx[m, f, l, :rows] = tile
                ym[g] = put_slot(ym[g], tile, l)
                hm[g * levels + l] = tile[:H]
                tm[g * levels + l] = tile[rows - H :]
            sums[l, f] = total
        tile = d_ref[l]
        dx[l, :rows] = tile
        ym[base] = put_slot(ym[base], tile, l)
        hm[base * levels + l] = tile[:H]
        tm[base * levels + l] = tile[rows - H :]

    tile = r_ref[...]
    rx[:rows] = tile
    ym[base + 1] = put_slot(jnp.zeros((rows, LANES), F32), tile, 0)
    hm[(base + 1) * levels] = tile[:H]
    tm[(base + 1) * levels] = tile[rows - H :]
    got_ym = send_y(ym, ym_in)
    got_xm = send_x(hm, tm, nm, prm)
    got_sum = []
    for k in range(1, n):
        owner = lax.rem(me + k, n)
        got_sum.append(send(sums.at[pl.ds(owner * clevels, clevels)], sums_in.at[k - 1], peers[k - 1]))

    landed(got_yc)
    got_cc = send_corners(yc_in, ccor, ccor_in)
    landed(got_xc)
    landed(got_cc)

    def side_values(body, corners, g):
        out = [
            jnp.concatenate([body[s, g], corners[s, 0, g], corners[s, 1, g]], axis=0)
            for s in range(nsides)
        ]
        return out[0], out[-1]

    half_x, half_y = crows // 2, ccols // 2
    height, full = crows + 2 * H, ccols + LANES

    def control_level(l):
        left, right = side_values(yc_in, ccor_in, 0)
        body = []
        for f in range(fields):
            t = f * clevels + l
            own = jnp.concatenate([c_ref[f, l], nc[t], prc[t]], axis=0)
            body.append(jnp.concatenate([own, side_block(left, right, t)], axis=1))
        for _ in range(CSTEPS):
            a = body[0] * (0.5 * step_control)
            b = body[1] * (0.5 * step_control)
            new = []
            for f in body:
                ux = pltpu.roll(f, height - 1, 0)
                lx = pltpu.roll(f, 1, 0)
                uy = pltpu.roll(f, full - 1, 1)
                ly = pltpu.roll(f, 1, 1)
                lap = (ux + lx) + (uy + ly) - 4.0 * f
                new.append(f + ((step_control * viscosity) * lap - a * (ux - lx) - b * (uy - ly)))
            body = new
        pick_y = (
            lax.broadcasted_iota(jnp.int32, (ccols, half_y), 0) // 2
            == lax.broadcasted_iota(jnp.int32, (ccols, half_y), 1)
        ).astype(F32)
        pick_x = (
            lax.broadcasted_iota(jnp.int32, (half_x, crows), 1) // 2
            == lax.broadcasted_iota(jnp.int32, (half_x, crows), 0)
        ).astype(F32)
        for f in range(fields):
            field = body[f][:crows, :ccols]
            cf_ref[f, l] = field
            t = jnp.dot(field, pick_y, precision=lax.Precision.HIGHEST, preferred_element_type=F32)
            t = jnp.dot(pick_x, t, precision=lax.Precision.HIGHEST, preferred_element_type=F32)
            corr[l, f] = 0.25 * t

    pl.loop(0, 1)(control_level)
    landed(got_ym)
    got_mc = send_corners(ym_in, mcor, mcor_in)
    pl.loop(1, clevels)(control_level)
    landed(got_sum)

    @pl.loop(0, clevels)
    def _(l):
        for f in range(fields):
            total = sums[me * clevels + l, f]
            for k in range(n - 1):
                total = total + sums_in[k, l, f]
            tile = corr[l, f] - total * (1.0 / (count * n))
            kx[l, f, :rows] = tile
            ycorr[f] = put_slot(ycorr[f], tile, me * clevels + l)
            hcorr[f * clevels + l] = tile[:H]
            tcorr[f * clevels + l] = tile[rows - H :]

    got_yk = send_y(ycorr, ycorr_in)
    got_xk = send_x(hcorr, tcorr, ncorr, prcorr)
    landed(got_xm)
    landed(got_mc)

    height = rows + 2 * H
    stride = height // 8
    side = lax.rem(lane_ids(height), SLOT)

    def load(ref, *at):
        return jnp.concatenate(
            [ref[(*at, pl.ds(i, 8, stride=stride), slice(None))] for i in range(stride)], axis=0
        )

    def store(ref, value, *at):
        for i in range(stride):
            kept = (rows - i + stride - 1) // stride
            ref[(*at, pl.ds(i, kept, stride=stride), slice(None))] = value[8 * i : 8 * i + kept]

    def up_x(f):
        return jnp.concatenate([f[8:], pltpu.roll(f[:8], 7, 0)], axis=0)

    def low_x(f):
        return jnp.concatenate([pltpu.roll(f[-8:], 1, 0), f[:-8]], axis=0)

    def split(f):
        high = f.astype(jnp.bfloat16)
        return high, f - high.astype(F32)

    def row_ids(n):
        return lax.broadcasted_iota(jnp.int32, (n, 2 * LANES), 0)

    def column_ids(n):
        return lax.broadcasted_iota(jnp.int32, (n, 2 * LANES), 1)

    def ones(mask):
        return jnp.where(mask, 1.0, 0.0)

    r, c = lax.rem(row_ids(2 * LANES), LANES), column_ids(2 * LANES)
    up = (c < LANES) & (r == c + 1)
    low = (c > LANES) & (r == c - LANES - 1)
    wtop[...] = (ones(up | low) - ones(r == lax.rem(c, LANES))).astype(jnp.bfloat16)
    last = (levels // 2 - 1) * 2 * SLOT
    for parity in range(2):
        r, c = row_ids(wbot.shape[1]) - (last + SLOT * parity), column_ids(wbot.shape[1])
        up = (c == LANES - 1) & ((r == H) | (r == H + 2))
        low = (c == LANES) & ((r == H - 1) | (r == H + 1))
        wbot[parity] = ones(up | low).astype(jnp.bfloat16)

    def product(parts, right):
        return jnp.dot(jnp.concatenate(parts, axis=1), right, preferred_element_type=F32)

    def weights_of(l):
        start = pl.multiple_of(last - 2 * SLOT * (l // 2), 2 * SLOT)
        return jnp.concatenate([wtop[...], wbot[lax.rem(l, 2), pl.ds(start, LANES), :]], axis=0)

    def inner(high, low):
        before, after = high[:height].astype(F32), high[height:].astype(F32)
        rest = pltpu.roll(jnp.where(side == H - 1, low[:height], low[height:]), 2, 1)
        return jnp.where(side == H - 1, before, jnp.where(side == H, after, rest))

    def move(f, d, east, north, south):
        fx = east * (up_x(f) - f)
        return (f + north * d[:, :LANES]) + (south * d[:, LANES:] + (fx - low_x(fx)))

    def evolve_strips(ref, p_at, q_at, out, at):
        fields_of = [
            jnp.concatenate([load(ref, s, g) for s in range(2)], axis=0) for g in (p_at, q_at)
        ]
        for step in range(MSTEPS):
            parts = [split(f) for f in fields_of]
            out[(*at, step)] = jnp.concatenate(
                [inner(*part) for part in parts], axis=0
            ).astype(jnp.bfloat16)
            if step == MSTEPS - 1:
                break
            moved = []
            for f, (high, low) in zip(fields_of, parts):
                d = product([high, low.astype(jnp.bfloat16)], wtop[...])
                new = []
                for s in range(2):
                    part = slice(s * height, (s + 1) * height)
                    new.append(move(f[part], d[part], *[edge_coef[s, k] for k in range(3)]))
                moved.append(jnp.concatenate(new, axis=0))
            spin = jnp.concatenate([edge_coef[s, 3] for s in range(2)], axis=0)
            p, q = fields_of
            fields_of = [moved[0] - spin * q, moved[1] + spin * p]

    def pack_strips(own, halo, body, corners, g, out, at):
        own = jnp.concatenate([own, halo], axis=0)
        sides = side_values(body, corners, g)
        out[0, at] = jnp.where(side < H, sides[0], own)
        out[1, at] = jnp.where(side < H, own, sides[1])

    def load_halos():
        ih[...] = jnp.zeros_like(ih)

        @pl.loop(0, levels)
        def _(l):
            for g in range(base + 1):
                t = g * levels + l
                halo = jnp.concatenate([nm[t], prm[t]], axis=0)
                ih[g] = put_slot(ih[g], halo, l)
                if g == base:
                    dx[l, rows:] = halo
                else:
                    mx[g // fields, g % fields, l, rows:] = halo

        t = (base + 1) * levels
        halo = jnp.concatenate([nm[t], prm[t]], axis=0)
        rx[rows:] = halo
        ih[base + 1] = put_slot(ih[base + 1], halo, 0)
        for g in range(base + 2):
            pack_strips(ym[g], ih[g], ym_in, mcor_in, g, strips, g)
        kappa = jnp.concatenate([load(strips, s, base) for s in range(2)], axis=0)
        high, low = split(kappa)
        high_low = product([high, low.astype(jnp.bfloat16)], wtop[...])
        khalo[...] = jnp.concatenate([inner(high, low), jnp.zeros((8, LANES), F32)], axis=0).astype(jnp.bfloat16)
        for s in range(2):
            part = slice(s * height, (s + 1) * height)
            f, d = kappa[part], high_low[part]
            edge_coef[s, 0] = (0.5 * step_member) * (f + up_x(f))
            edge_coef[s, 1] = step_member * f + (0.5 * step_member) * d[:, :LANES]
            edge_coef[s, 2] = step_member * f + (0.5 * step_member) * d[:, LANES:]
            spin = load(strips, s, base + 1)
            spin = jnp.where(lane_ids(height) < SLOT, step_member * spin, 0.0)
            width = SLOT
            while width < LANES:
                spin = spin + pltpu.roll(spin, width, 1)
                width *= 2
            edge_coef[s, 3] = spin
        for m in range(count):
            evolve_strips(strips, m * fields, m * fields + 1, halos, (m,))

    def coefficients(l, right):
        kappa = load(dx, l)
        high, low = split(jnp.concatenate([kappa, jnp.zeros((8, LANES), F32)], axis=0))
        d = product([high, low.astype(jnp.bfloat16), khalo[...]], right)[:height]
        east = (0.5 * step_member) * (kappa + up_x(kappa))
        north = step_member * kappa + (0.5 * step_member) * d[:, :LANES]
        south = step_member * kappa + (0.5 * step_member) * d[:, LANES:]
        return east, north, south, step_member * load(rx)

    def steps(p, q, halo, at, right, east, north, south, spin):
        for step in range(MSTEPS):
            high, low = split(jnp.concatenate([p, q], axis=0))
            d = product([high, low.astype(jnp.bfloat16), halo[(*at, step)]], right)
            moved = [
                move(f, d[k * height : (k + 1) * height], east, north, south)
                for k, f in enumerate((p, q))
            ]
            p, q = moved[0] - spin * q, moved[1] + spin * p
        return p, q

    def member_level(l):
        right = weights_of(l)
        w = coefficients(l, right)
        for m in range(count):
            p, q = steps(load(mx, m, 0, l), load(mx, m, 1, l), halos, (m,), right, *w)
            store(mf_ref, p, m, 0, l)
            store(mf_ref, q, m, 1, l)

    def load_correction_halos():
        kih[...] = jnp.zeros_like(kih)

        @pl.loop(0, clevels)
        def _(l):
            for f in range(fields):
                t = f * clevels + l
                halo = jnp.concatenate([ncorr[t], prcorr[t]], axis=0)
                kih[f] = put_slot(kih[f], halo, me * clevels + l)
                kx[l, f, rows:] = halo

        for f in range(fields):
            pack_strips(ycorr[f], kih[f], ycorr_in, kcor_in, f, kstrips, f)
        evolve_strips(kstrips, 0, 1, halos, (count,))

    def correction_level(l):
        right = weights_of(me * clevels + l)
        w = coefficients(me * clevels + l, right)
        p, q = steps(load(kx, l, 0), load(kx, l, 1), halos, (count,), right, *w)
        store(shift, p, l, 0)
        store(shift, q, l, 1)

    load_halos()
    cut_a, cut_b = (3 * levels) // 16, (6 * levels) // 16
    pl.loop(0, cut_a)(member_level)
    landed(got_yk)
    got_kc = send_corners(ycorr_in, kcor, kcor_in)
    pl.loop(cut_a, cut_b)(member_level)
    landed(got_xk)
    landed(got_kc)
    load_correction_halos()
    pl.loop(0, clevels)(correction_level)
    got_shift = [send(shift, shift_in.at[k], peers[k]) for k in range(n - 1)]
    pl.loop(cut_b, levels)(member_level)

    def add(piece, owner):
        @pl.loop(0, clevels)
        def _(l):
            for f in range(fields):
                tile = piece[l, f]
                for m in range(count):
                    at = owner * clevels + l
                    mf_ref[m, f, at] = mf_ref[m, f, at] + tile

    add(shift, me)
    for k in range(n - 1):
        landed([got_shift[k]])
        add(shift_in.at[k], lax.rem(me + n - 1 - k, n))
    for copy in pending:
        copy.wait_send()
    assert len(pending) == copies


def per_device(control, members, diffusivity, rotation):
    fields, clevels, crows, ccols = control.shape
    count, _, levels, rows, cols = members.shape
    base = count * fields
    tiles = (base + 1) * levels + 1
    n = lax.axis_size("mem")
    ns = 2 if lax.axis_size("gy") > 2 else 1
    copies = 3 * (ns + 2 + 2 * ns) + 2 * (n - 1)
    vmem = lambda *shape: pltpu.VMEM(shape, F32)
    narrow = lambda *shape: pltpu.VMEM(shape, jnp.bfloat16)
    height = rows + 2 * H
    scratch = (
        [vmem(fields * clevels, H, ccols)] * 4
        + [vmem(tiles, H, cols)] * 4
        + [vmem(1, crows, LANES), vmem(base + 2, rows, LANES)]
        + [vmem(ns, 1, crows, LANES), vmem(ns, base + 2, rows, LANES)]
        + [vmem(ns, 2, 1, H, LANES), vmem(ns, 2, base + 2, H, LANES)] * 2
        + [vmem(levels, fields, rows, cols), vmem(n - 1, clevels, fields, rows, cols)]
        + [vmem(clevels, fields, rows, cols)]
        + [vmem(fields * clevels, H, cols)] * 4
        + [vmem(fields, rows, LANES), vmem(ns, fields, rows, LANES)]
        + [vmem(ns, 2, fields, H, LANES)] * 2
        + [vmem(clevels, fields, rows, cols), vmem(n - 1, clevels, fields, rows, cols)]
        + [vmem(count, fields, levels, height, cols), vmem(levels, height, cols), vmem(height, cols)]
        + [vmem(clevels, fields, height, cols), vmem(base + 2, 2 * H, cols), vmem(fields, 2 * H, cols)]
        + [vmem(2, base + 2, height, cols), vmem(2, fields, height, cols), vmem(2, 4, height, cols)]
        + [narrow(count + 1, MSTEPS, fields * height, cols), narrow(height + 8, cols)]
        + [narrow(2 * LANES, 2 * LANES), narrow(2, LANES + SLOT * levels, 2 * LANES)]
        + [pltpu.SemaphoreType.DMA((copies,))] * 2
    )
    return pl.pallas_call(
        functools.partial(fused_kernel, copies),
        in_specs=[pl.BlockSpec(memory_space=pltpu.VMEM)] * 4,
        out_specs=[pl.BlockSpec(memory_space=pltpu.VMEM)] * 2,
        out_shape=[
            jax.ShapeDtypeStruct(control.shape, F32),
            jax.ShapeDtypeStruct(members.shape, F32),
        ],
        scratch_shapes=scratch,
        compiler_params=pltpu.CompilerParams(collective_id=0, has_side_effects=True),
        name="fused",
    )(control, members, diffusivity, rotation)


def solution(mesh):
    in_specs = (
        P(None, "mem", "gx", "gy"),
        P("mem", None, None, "gx", "gy"),
        P(None, "gx", "gy"),
        P("gx", "gy"),
    )
    out_specs = (P(None, "mem", "gx", "gy"), P("mem", None, None, "gx", "gy"))
    return jax.shard_map(
        per_device, mesh=mesh, in_specs=in_specs, out_specs=out_specs, check_vma=False
    )
```

```python
import functools

import jax
import jax.numpy as jnp
from jax import lax
from jax.experimental import pallas as pl
from jax.experimental.pallas import tpu as pltpu
from jax.sharding import PartitionSpec as P

CSTEPS = 4
MSTEPS = 4
H = 4
SLOT = 2 * H
LANES = 128

step_control = 0.15
viscosity = 0.5
step_member = 0.5
F32 = jnp.float32


def lane_ids(rows):
    return lax.broadcasted_iota(jnp.int32, (rows, LANES), 1)


def to_slot(edges, slot):
    shift = H + SLOT * slot
    if not isinstance(slot, int):
        shift = lax.rem(shift, LANES)
    return pltpu.roll(edges, shift, 1)


def merge_slot(packed, rolled, slot):
    ids = lane_ids(rolled.shape[0])
    inside = (ids >= SLOT * slot) & (ids < SLOT * slot + SLOT)
    return jnp.where(inside, rolled, packed)


def put_slot(packed, edges, slot):
    return merge_slot(packed, to_slot(edges, slot), slot)


def side_block(left, right, slot):
    shift = lax.rem(2 * LANES - SLOT * slot - H, LANES)
    after = pltpu.roll(right, shift, 1)
    if left is right:
        return after
    before = pltpu.roll(left, shift, 1)
    return jnp.where(lane_ids(after.shape[0]) < LANES // 2, after, before)


def fused_kernel(
    copies, c_ref, m_ref, d_ref, r_ref, cf_ref, mf_ref,
    hc, tc, nc, prc, hm, tm, nm, prm, yc, ym, yc_in, ym_in, ccor, mcor, ccor_in, mcor_in,
    sums, sums_in, corr, hcorr, tcorr, ncorr, prcorr, ycorr, ycorr_in, kcor, kcor_in,
    shift, shift_in, mx, dx, rx, kx, ih, kih, strips, kstrips, edge_coef, halos, khalo,
    send_sem, recv_sem,
):
    fields, clevels, crows, ccols = c_ref.shape
    count, _, levels, rows, cols = m_ref.shape
    base = count * fields
    nx, ny, n = lax.axis_size("gx"), lax.axis_size("gy"), lax.axis_size("mem")
    x, y, me = lax.axis_index("gx"), lax.axis_index("gy"), lax.axis_index("mem")
    two = ny > 2
    nsides = 2 if two else 1
    x_next, x_prev = {"gx": lax.rem(x + 1, nx)}, {"gx": lax.rem(x + nx - 1, nx)}
    y_next, y_prev = {"gy": lax.rem(y + 1, ny)}, {"gy": lax.rem(y + ny - 1, ny)}
    peers = [{"mem": lax.rem(me + k, n)} for k in range(1, n)]
    mesh_id = pl.DeviceIdType.MESH
    pending = []

    def send(src, dst, target):
        k = len(pending)
        copy = pltpu.make_async_remote_copy(
            src_ref=src, dst_ref=dst, send_sem=send_sem.at[k], recv_sem=recv_sem.at[k],
            device_id=target, device_id_type=mesh_id,
        )
        copy.start()
        pending.append(copy)
        return copy

    def landed(group):
        for copy in group:
            copy.wait_recv()

    def send_y(src, dst):
        group = [send(src, dst.at[0], y_next)]
        if two:
            group.append(send(src, dst.at[1], y_prev))
        return group

    def send_x(first, last, from_next, from_prev):
        return [send(first, from_next, x_prev), send(last, from_prev, x_next)]

    def send_corners(got, buf, buf_in):
        group = []
        for side in range(nsides):
            for g in range(got.shape[1]):
                tile = got[side, g]
                buf[side, 0, g] = tile[:H]
                buf[side, 1, g] = tile[tile.shape[0] - H :]
            group += send_x(
                buf.at[side, 0], buf.at[side, 1], buf_in.at[side, 0], buf_in.at[side, 1]
            )
        return group

    barrier = pltpu.get_barrier_semaphore()
    greeted = [x_next, x_prev, y_next] + ([y_prev] if two else []) + peers
    for target in greeted:
        pl.semaphore_signal(barrier, inc=1, device_id=target, device_id_type=mesh_id)

    ids = lane_ids(crows)
    yc[...] = jnp.zeros_like(yc)
    ym[...] = jnp.zeros_like(ym)
    ycorr[...] = jnp.zeros_like(ycorr)

    @pl.loop(0, clevels)
    def _(l):
        for f in range(fields):
            first = c_ref[f, l, :, :LANES]
            last = c_ref[f, l, :, ccols - LANES :]
            t = f * clevels + l
            yc[0] = put_slot(yc[0], jnp.where(ids < LANES // 2, first, last), t)
            hc[t] = c_ref[f, l, :H]
            tc[t] = c_ref[f, l, crows - H :]

    pl.semaphore_wait(barrier, len(greeted))
    got_yc = send_y(yc, yc_in)
    got_xc = send_x(hc, tc, nc, prc)

    @pl.loop(0, levels)
    def _(l):
        for f in range(fields):
            total = None
            for m in range(count):
                tile = m_ref[m, f, l]
                total = tile if total is None else total + tile
                g = m * fields + f
                rolled = to_slot(tile, l)
                mx[m, f, l, :rows] = rolled
                ym[g] = merge_slot(ym[g], rolled, l)
                hm[g * levels + l] = tile[:H]
                tm[g * levels + l] = tile[rows - H :]
            sums[l, f] = total
        tile = d_ref[l]
        rolled = to_slot(tile, l)
        dx[l, :rows] = rolled
        ym[base] = merge_slot(ym[base], rolled, l)
        hm[base * levels + l] = tile[:H]
        tm[base * levels + l] = tile[rows - H :]

    tile = r_ref[...]
    rolled = to_slot(tile, 0)
    rx[:rows] = rolled
    ym[base + 1] = merge_slot(jnp.zeros((rows, LANES), F32), rolled, 0)
    hm[(base + 1) * levels] = tile[:H]
    tm[(base + 1) * levels] = tile[rows - H :]
    got_ym = send_y(ym, ym_in)
    got_xm = send_x(hm, tm, nm, prm)
    got_sum = []
    for k in range(1, n):
        owner = lax.rem(me + k, n)
        got_sum.append(send(sums.at[pl.ds(owner * clevels, clevels)], sums_in.at[k - 1], peers[k - 1]))

    landed(got_yc)
    got_cc = send_corners(yc_in, ccor, ccor_in)
    landed(got_xc)
    landed(got_cc)

    def side_values(body, corners, g):
        out = [
            jnp.concatenate([body[s, g], corners[s, 0, g], corners[s, 1, g]], axis=0)
            for s in range(nsides)
        ]
        return out[0], out[-1]

    half_x, half_y = crows // 2, ccols // 2
    height, full = crows + 2 * H, ccols + LANES

    def control_level(l):
        left, right = side_values(yc_in, ccor_in, 0)
        body = []
        for f in range(fields):
            t = f * clevels + l
            own = jnp.concatenate([c_ref[f, l], nc[t], prc[t]], axis=0)
            body.append(jnp.concatenate([own, side_block(left, right, t)], axis=1))
        for _ in range(CSTEPS):
            a = body[0] * (0.5 * step_control)
            b = body[1] * (0.5 * step_control)
            new = []
            for f in body:
                ux = pltpu.roll(f, height - 1, 0)
                lx = pltpu.roll(f, 1, 0)
                uy = pltpu.roll(f, full - 1, 1)
                ly = pltpu.roll(f, 1, 1)
                lap = (ux + lx) + (uy + ly) - 4.0 * f
                new.append(f + ((step_control * viscosity) * lap - a * (ux - lx) - b * (uy - ly)))
            body = new
        pick_y = (
            lax.broadcasted_iota(jnp.int32, (ccols, half_y), 0) // 2
            == lax.broadcasted_iota(jnp.int32, (ccols, half_y), 1)
        ).astype(F32)
        pick_x = (
            lax.broadcasted_iota(jnp.int32, (half_x, crows), 1) // 2
            == lax.broadcasted_iota(jnp.int32, (half_x, crows), 0)
        ).astype(F32)
        for f in range(fields):
            field = body[f][:crows, :ccols]
            cf_ref[f, l] = field
            t = jnp.dot(field, pick_y, precision=lax.Precision.HIGHEST, preferred_element_type=F32)
            t = jnp.dot(pick_x, t, precision=lax.Precision.HIGHEST, preferred_element_type=F32)
            corr[l, f] = 0.25 * t

    pl.loop(0, 1)(control_level)
    landed(got_ym)
    got_mc = send_corners(ym_in, mcor, mcor_in)
    pl.loop(1, clevels)(control_level)
    landed(got_sum)

    @pl.loop(0, clevels)
    def _(l):
        for f in range(fields):
            total = sums[me * clevels + l, f]
            for k in range(n - 1):
                total = total + sums_in[k, l, f]
            tile = corr[l, f] - total * (1.0 / (count * n))
            rolled = to_slot(tile, me * clevels + l)
            kx[l, f, :rows] = rolled
            ycorr[f] = merge_slot(ycorr[f], rolled, me * clevels + l)
            hcorr[f * clevels + l] = tile[:H]
            tcorr[f * clevels + l] = tile[rows - H :]

    got_yk = send_y(ycorr, ycorr_in)
    got_xk = send_x(hcorr, tcorr, ncorr, prcorr)
    landed(got_xm)
    landed(got_mc)

    height = rows + 2 * H
    stride = height // 8
    side = lax.rem(lane_ids(height), SLOT)

    def load(ref, *at):
        return jnp.concatenate(
            [ref[(*at, pl.ds(i, 8, stride=stride), slice(None))] for i in range(stride)], axis=0
        )

    def store(ref, value, *at):
        for i in range(stride):
            kept = (rows - i + stride - 1) // stride
            ref[(*at, pl.ds(i, kept, stride=stride), slice(None))] = value[8 * i : 8 * i + kept]

    def up_x(f):
        return jnp.concatenate([f[8:], pltpu.roll(f[:8], 7, 0)], axis=0)

    def low_x(f):
        return jnp.concatenate([pltpu.roll(f[-8:], 1, 0), f[:-8]], axis=0)

    ids_m = lane_ids(height)

    def move(f, after, before, east, north, south):
        fx = east * (up_x(f) - f)
        return (f + north * (after - f)) + (south * (before - f) + (fx - low_x(fx)))

    def neighbours(f):
        return pltpu.roll(f, LANES - 1, 1), pltpu.roll(f, 1, 1)

    def joined(pair):
        return jnp.where(side == H - 1, pair[0], pair[1])

    def evolve_strips(ref, p_at, q_at, at):
        now = [[load(ref, s, g) for s in range(2)] for g in (p_at, q_at)]
        for step in range(MSTEPS):
            for f in range(2):
                halos[at, step, f] = joined(now[f])
            if step == MSTEPS - 1:
                break
            new = [[], []]
            for s in range(2):
                w = [edge_coef[s, k] for k in range(4)]
                p, q = [move(f[s], *neighbours(f[s]), *w[:3]) for f in now]
                new[0].append(p - w[3] * now[1][s])
                new[1].append(q + w[3] * now[0][s])
            now = new

    def pack_strips(own, halo, body, corners, g, out, at):
        own = jnp.concatenate([own, halo], axis=0)
        sides = side_values(body, corners, g)
        out[0, at] = jnp.where(side < H, sides[0], own)
        out[1, at] = jnp.where(side < H, own, sides[1])

    def load_halos():
        ih[...] = jnp.zeros_like(ih)

        @pl.loop(0, levels)
        def _(l):
            for g in range(base + 1):
                t = g * levels + l
                halo = to_slot(jnp.concatenate([nm[t], prm[t]], axis=0), l)
                ih[g] = merge_slot(ih[g], halo, l)
                if g == base:
                    dx[l, rows:] = halo
                else:
                    mx[g // fields, g % fields, l, rows:] = halo

        t = (base + 1) * levels
        halo = to_slot(jnp.concatenate([nm[t], prm[t]], axis=0), 0)
        rx[rows:] = halo
        ih[base + 1] = merge_slot(ih[base + 1], halo, 0)
        for g in range(base + 2):
            pack_strips(ym[g], ih[g], ym_in, mcor_in, g, strips, g)
        kappa = [load(strips, s, base) for s in range(2)]
        khalo[...] = joined(kappa)
        for s in range(2):
            f = kappa[s]
            after, before = neighbours(f)
            edge_coef[s, 0] = (0.5 * step_member) * (f + up_x(f))
            edge_coef[s, 1] = (0.5 * step_member) * (f + after)
            edge_coef[s, 2] = (0.5 * step_member) * (f + before)
            spin = jnp.where(ids_m < SLOT, step_member * load(strips, s, base + 1), 0.0)
            width = SLOT
            while width < LANES:
                spin = spin + pltpu.roll(spin, width, 1)
                width *= 2
            edge_coef[s, 3] = spin
        for m in range(count):
            evolve_strips(strips, m * fields, m * fields + 1, m)

    def evolve(pairs, at, l):
        first = SLOT * l + H
        is_first, is_last = ids_m == first, ids_m == first - 1

        def beside(f, halo):
            after = pltpu.roll(jnp.where(is_first, halo, f), LANES - 1, 1)
            before = pltpu.roll(jnp.where(is_last, halo, f), 1, 1)
            return after, before

        kappa = load(dx, l)
        after, before = beside(kappa, khalo[...])
        east = (0.5 * step_member) * (kappa + up_x(kappa))
        north = (0.5 * step_member) * (kappa + after)
        south = (0.5 * step_member) * (kappa + before)
        spin = step_member * pltpu.roll(load(rx), SLOT * l, 1)
        out = []
        for (p, q), m in zip(pairs, at):
            for step in range(MSTEPS):
                moved = [
                    move(f, *beside(f, halos[m, step, k]), east, north, south)
                    for k, f in enumerate((p, q))
                ]
                p, q = moved[0] - spin * q, moved[1] + spin * p
            out += [pltpu.roll(f, LANES - first, 1) for f in (p, q)]
        return out

    def member_level(l):
        pairs = [[load(mx, m, f, l) for f in range(fields)] for m in range(count)]
        for k, value in enumerate(evolve(pairs, range(count), l)):
            store(mf_ref, value, k // fields, k % fields, l)

    def load_correction_halos():
        kih[...] = jnp.zeros_like(kih)

        @pl.loop(0, clevels)
        def _(l):
            for f in range(fields):
                t = f * clevels + l
                halo = to_slot(jnp.concatenate([ncorr[t], prcorr[t]], axis=0), me * clevels + l)
                kih[f] = merge_slot(kih[f], halo, me * clevels + l)
                kx[l, f, rows:] = halo

        for f in range(fields):
            pack_strips(ycorr[f], kih[f], ycorr_in, kcor_in, f, kstrips, f)
        evolve_strips(kstrips, 0, 1, count)

    def correction_level(l):
        pair = [load(kx, l, f) for f in range(fields)]
        for f, value in enumerate(evolve([pair], [count], me * clevels + l)):
            store(shift, value, l, f)

    load_halos()
    cut_a, cut_b = (3 * levels) // 16, (6 * levels) // 16
    pl.loop(0, cut_a)(member_level)
    landed(got_yk)
    got_kc = send_corners(ycorr_in, kcor, kcor_in)
    pl.loop(cut_a, cut_b)(member_level)
    landed(got_xk)
    landed(got_kc)
    load_correction_halos()
    pl.loop(0, clevels)(correction_level)
    got_shift = [send(shift, shift_in.at[k], peers[k]) for k in range(n - 1)]
    pl.loop(cut_b, levels)(member_level)

    def add(piece, owner):
        @pl.loop(0, clevels)
        def _(l):
            for f in range(fields):
                tile = piece[l, f]
                for m in range(count):
                    at = owner * clevels + l
                    mf_ref[m, f, at] = mf_ref[m, f, at] + tile

    add(shift, me)
    for k in range(n - 1):
        landed([got_shift[k]])
        add(shift_in.at[k], lax.rem(me + n - 1 - k, n))
    for copy in pending:
        copy.wait_send()
    assert len(pending) == copies


def per_device(control, members, diffusivity, rotation):
    fields, clevels, crows, ccols = control.shape
    count, _, levels, rows, cols = members.shape
    base = count * fields
    tiles = (base + 1) * levels + 1
    n = lax.axis_size("mem")
    ns = 2 if lax.axis_size("gy") > 2 else 1
    copies = 3 * (ns + 2 + 2 * ns) + 2 * (n - 1)
    vmem = lambda *shape: pltpu.VMEM(shape, F32)
    height = rows + 2 * H
    scratch = (
        [vmem(fields * clevels, H, ccols)] * 4
        + [vmem(tiles, H, cols)] * 4
        + [vmem(1, crows, LANES), vmem(base + 2, rows, LANES)]
        + [vmem(ns, 1, crows, LANES), vmem(ns, base + 2, rows, LANES)]
        + [vmem(ns, 2, 1, H, LANES), vmem(ns, 2, base + 2, H, LANES)] * 2
        + [vmem(levels, fields, rows, cols), vmem(n - 1, clevels, fields, rows, cols)]
        + [vmem(clevels, fields, rows, cols)]
        + [vmem(fields * clevels, H, cols)] * 4
        + [vmem(fields, rows, LANES), vmem(ns, fields, rows, LANES)]
        + [vmem(ns, 2, fields, H, LANES)] * 2
        + [vmem(clevels, fields, rows, cols), vmem(n - 1, clevels, fields, rows, cols)]
        + [vmem(count, fields, levels, height, cols), vmem(levels, height, cols), vmem(height, cols)]
        + [vmem(clevels, fields, height, cols), vmem(base + 2, 2 * H, cols), vmem(fields, 2 * H, cols)]
        + [vmem(2, base + 2, height, cols), vmem(2, fields, height, cols), vmem(2, 4, height, cols)]
        + [vmem(count + 1, MSTEPS, fields, height, cols), vmem(height, cols)]
        + [pltpu.SemaphoreType.DMA((copies,))] * 2
    )
    return pl.pallas_call(
        functools.partial(fused_kernel, copies),
        in_specs=[pl.BlockSpec(memory_space=pltpu.VMEM)] * 4,
        out_specs=[pl.BlockSpec(memory_space=pltpu.VMEM)] * 2,
        out_shape=[
            jax.ShapeDtypeStruct(control.shape, F32),
            jax.ShapeDtypeStruct(members.shape, F32),
        ],
        scratch_shapes=scratch,
        compiler_params=pltpu.CompilerParams(collective_id=0, has_side_effects=True),
        name="fused",
    )(control, members, diffusivity, rotation)


def solution(mesh):
    in_specs = (
        P(None, "mem", "gx", "gy"),
        P("mem", None, None, "gx", "gy"),
        P(None, "gx", "gy"),
        P("gx", "gy"),
    )
    out_specs = (P(None, "mem", "gx", "gy"), P("mem", None, None, "gx", "gy"))
    return jax.shard_map(
        per_device, mesh=mesh, in_specs=in_specs, out_specs=out_specs, check_vma=False
    )
```

```python
import functools

import jax
import jax.numpy as jnp
from jax import lax
from jax.experimental import pallas as pl
from jax.experimental.pallas import tpu as pltpu
from jax.sharding import PartitionSpec as P

CSTEPS = 4
MSTEPS = 4
H = 4
SLOT = 2 * H
LANES = 128

step_control = 0.15
viscosity = 0.5
step_member = 0.5
F32 = jnp.float32


def lane_ids(rows):
    return lax.broadcasted_iota(jnp.int32, (rows, LANES), 1)


def to_slot(edges, slot):
    shift = H + SLOT * slot
    if not isinstance(slot, int):
        shift = lax.rem(shift, LANES)
    return pltpu.roll(edges, shift, 1)


def merge_slot(packed, rolled, slot):
    ids = lane_ids(rolled.shape[0])
    inside = (ids >= SLOT * slot) & (ids < SLOT * slot + SLOT)
    return jnp.where(inside, rolled, packed)


def put_slot(packed, edges, slot):
    return merge_slot(packed, to_slot(edges, slot), slot)


def side_block(left, right, slot):
    shift = lax.rem(2 * LANES - SLOT * slot - H, LANES)
    after = pltpu.roll(right, shift, 1)
    if left is right:
        return after
    before = pltpu.roll(left, shift, 1)
    return jnp.where(lane_ids(after.shape[0]) < LANES // 2, after, before)


def fused_kernel(
    copies, c_ref, m_ref, d_ref, r_ref, cf_ref, mf_ref,
    hc, tc, nc, prc, hm, tm, nm, prm, yc, ym, yc_in, ym_in, ccor, mcor, ccor_in, mcor_in,
    sums, sums_in, corr, hcorr, tcorr, ncorr, prcorr, ycorr, ycorr_in, kcor, kcor_in,
    shift, shift_in, mx, dx, rx, kx, ih, kih, strips, kstrips, edge_coef, halos, khalo, part,
    send_sem, recv_sem,
):
    fields, clevels, crows, ccols = c_ref.shape
    count, _, levels, rows, cols = m_ref.shape
    base = count * fields
    nx, ny, n = lax.axis_size("gx"), lax.axis_size("gy"), lax.axis_size("mem")
    x, y, me = lax.axis_index("gx"), lax.axis_index("gy"), lax.axis_index("mem")
    two = ny > 2
    nsides = 2 if two else 1
    x_next, x_prev = {"gx": lax.rem(x + 1, nx)}, {"gx": lax.rem(x + nx - 1, nx)}
    y_next, y_prev = {"gy": lax.rem(y + 1, ny)}, {"gy": lax.rem(y + ny - 1, ny)}
    peers = [{"mem": lax.rem(me + k, n)} for k in range(1, n)]
    mesh_id = pl.DeviceIdType.MESH
    pending = []

    def send(src, dst, target):
        k = len(pending)
        copy = pltpu.make_async_remote_copy(
            src_ref=src, dst_ref=dst, send_sem=send_sem.at[k], recv_sem=recv_sem.at[k],
            device_id=target, device_id_type=mesh_id,
        )
        copy.start()
        pending.append(copy)
        return copy

    def landed(group):
        for copy in group:
            copy.wait_recv()

    def send_y(src, dst):
        group = [send(src, dst.at[0], y_next)]
        if two:
            group.append(send(src, dst.at[1], y_prev))
        return group

    def send_x(first, last, from_next, from_prev):
        return [send(first, from_next, x_prev), send(last, from_prev, x_next)]

    def send_corners(own, buf, buf_in):
        for g in range(own.shape[0]):
            tile = own[g]
            buf[0, g] = tile[:H]
            buf[1, g] = tile[tile.shape[0] - H :]
        group = []
        for k, across in enumerate([y_next] + ([y_prev] if two else [])):
            group.append(send(buf.at[0], buf_in.at[k, 0], {**x_prev, **across}))
            group.append(send(buf.at[1], buf_in.at[k, 1], {**x_next, **across}))
        return group

    barrier = pltpu.get_barrier_semaphore()
    greeted = [x_next, x_prev, y_next] + ([y_prev] if two else []) + peers
    for across in [y_next] + ([y_prev] if two else []):
        greeted += [{**x_next, **across}, {**x_prev, **across}]
    for target in greeted:
        pl.semaphore_signal(barrier, inc=1, device_id=target, device_id_type=mesh_id)

    ids = lane_ids(crows)
    yc[...] = jnp.zeros_like(yc)
    ym[...] = jnp.zeros_like(ym)
    ycorr[...] = jnp.zeros_like(ycorr)

    @pl.loop(0, clevels)
    def _(l):
        for f in range(fields):
            first = c_ref[f, l, :, :LANES]
            last = c_ref[f, l, :, ccols - LANES :]
            t = f * clevels + l
            yc[0] = put_slot(yc[0], jnp.where(ids < LANES // 2, first, last), t)
            hc[t] = c_ref[f, l, :H]
            tc[t] = c_ref[f, l, crows - H :]

    @pl.loop(0, levels)
    def _(l):
        for f in range(fields):
            total = m_ref[0, f, l]
            for m in range(1, count):
                total = total + m_ref[m, f, l]
            sums[l, f] = total

    pl.semaphore_wait(barrier, len(greeted))
    got_yc = send_y(yc, yc_in)
    got_xc = send_x(hc, tc, nc, prc)
    got_cc = send_corners(yc, ccor, ccor_in)
    square = n == 4

    def piece(owner, *f):
        return sums.at[(pl.ds(owner * clevels, clevels), *f)]

    if square:
        owners = [me + 1 - 2 * lax.rem(me, 2), me + 2 - 4 * (me // 2), 3 - me]
        near = [{"mem": owners[0]}, {"mem": owners[1]}]
        got_far = [send(piece(owners[2], k), sums_in.at[2, :, k], near[k]) for k in range(2)]
        got_sum = [send(piece(owners[k], k), sums_in.at[k, :, k], near[k]) for k in range(2)]
    else:
        owners = [lax.rem(me + n - 1 - k, n) for k in range(n - 1)]
        got_sum = [
            send(piece(lax.rem(me + k, n)), sums_in.at[k - 1], peers[k - 1]) for k in range(1, n)
        ]

    @pl.loop(0, levels)
    def _(l):
        for f in range(fields):
            for m in range(count):
                tile = m_ref[m, f, l]
                g = m * fields + f
                rolled = to_slot(tile, l)
                mx[m, f, l, :rows] = rolled
                ym[g] = merge_slot(ym[g], rolled, l)
                hm[g * levels + l] = tile[:H]
                tm[g * levels + l] = tile[rows - H :]
        tile = d_ref[l]
        rolled = to_slot(tile, l)
        dx[l, :rows] = (0.5 * step_member) * rolled
        ym[base] = merge_slot(ym[base], rolled, l)
        hm[base * levels + l] = tile[:H]
        tm[base * levels + l] = tile[rows - H :]

    tile = r_ref[...]
    rolled = to_slot(tile, 0)
    rx[:rows] = step_member * rolled
    ym[base + 1] = merge_slot(jnp.zeros((rows, LANES), F32), rolled, 0)
    hm[(base + 1) * levels] = tile[:H]
    tm[(base + 1) * levels] = tile[rows - H :]
    got_ym = send_y(ym, ym_in)
    got_xm = send_x(hm, tm, nm, prm)
    got_mc = send_corners(ym, mcor, mcor_in)
    landed(got_yc)
    landed(got_xc)
    landed(got_cc)
    if square:
        for k in range(2):
            landed([got_far[k]])

            @pl.loop(0, clevels)
            def _(l):
                part[l, k] = sums[owners[1 - k] * clevels + l, k] + sums_in[2, l, k]

            got_sum.append(send(part.at[:, k], sums_in.at[1 - k, :, k], near[1 - k]))

    def side_values(body, corners, g):
        out = [
            jnp.concatenate([body[s, g], corners[s, 0, g], corners[s, 1, g]], axis=0)
            for s in range(nsides)
        ]
        return out[0], out[-1]

    half_x, half_y = crows // 2, ccols // 2
    height, full = crows + 2 * H, ccols + LANES

    def control_level(l):
        left, right = side_values(yc_in, ccor_in, 0)
        body = []
        for f in range(fields):
            t = f * clevels + l
            own = jnp.concatenate([c_ref[f, l], nc[t], prc[t]], axis=0)
            body.append(jnp.concatenate([own, side_block(left, right, t)], axis=1))
        for _ in range(CSTEPS):
            a = body[0] * (0.5 * step_control)
            b = body[1] * (0.5 * step_control)
            new = []
            for f in body:
                ux = pltpu.roll(f, height - 1, 0)
                lx = pltpu.roll(f, 1, 0)
                uy = pltpu.roll(f, full - 1, 1)
                ly = pltpu.roll(f, 1, 1)
                lap = (ux + lx) + (uy + ly) - 4.0 * f
                new.append(f + ((step_control * viscosity) * lap - a * (ux - lx) - b * (uy - ly)))
            body = new
        pick_y = (
            lax.broadcasted_iota(jnp.int32, (ccols, half_y), 0) // 2
            == lax.broadcasted_iota(jnp.int32, (ccols, half_y), 1)
        ).astype(F32)
        pick_x = (
            lax.broadcasted_iota(jnp.int32, (half_x, crows), 1) // 2
            == lax.broadcasted_iota(jnp.int32, (half_x, crows), 0)
        ).astype(F32)
        for f in range(fields):
            field = body[f][:crows, :ccols]
            cf_ref[f, l] = field
            t = jnp.dot(field, pick_y, precision=lax.Precision.HIGHEST, preferred_element_type=F32)
            t = jnp.dot(pick_x, t, precision=lax.Precision.HIGHEST, preferred_element_type=F32)
            corr[l, f] = 0.25 * t

    pl.loop(0, clevels)(control_level)
    landed(got_ym)
    height = rows + 2 * H
    stride = height // 8
    side = lax.rem(lane_ids(height), SLOT)

    def load(ref, *at):
        return jnp.concatenate(
            [ref[(*at, pl.ds(i, 8, stride=stride), slice(None))] for i in range(stride)], axis=0
        )

    def store(ref, value, *at):
        for i in range(stride):
            kept = (rows - i + stride - 1) // stride
            ref[(*at, pl.ds(i, kept, stride=stride), slice(None))] = value[8 * i : 8 * i + kept]

    def up_x(f):
        return jnp.concatenate([f[8:], pltpu.roll(f[:8], 7, 0)], axis=0)

    def low_x(f):
        return jnp.concatenate([pltpu.roll(f[-8:], 1, 0), f[:-8]], axis=0)

    ids_m = lane_ids(height)

    def move(f, after, before, east, north, south):
        fx = east * (up_x(f) - f)
        return (f + north * (after - f)) + (south * (before - f) + (fx - low_x(fx)))

    def neighbours(f):
        return pltpu.roll(f, LANES - 1, 1), pltpu.roll(f, 1, 1)

    def joined(pair):
        return jnp.where(side == H - 1, pair[0], pair[1])

    def evolve_strips(ref, p_at, q_at, at):
        now = [[load(ref, s, g) for s in range(2)] for g in (p_at, q_at)]
        for step in range(MSTEPS):
            for f in range(2):
                halos[at, step, f] = joined(now[f])
            if step == MSTEPS - 1:
                break
            new = [[], []]
            for s in range(2):
                w = [edge_coef[s, k] for k in range(4)]
                p, q = [move(f[s], *neighbours(f[s]), *w[:3]) for f in now]
                new[0].append(p - w[3] * now[1][s])
                new[1].append(q + w[3] * now[0][s])
            now = new

    def pack_strips(own, halo, body, corners, g, out, at):
        own = jnp.concatenate([own, halo], axis=0)
        sides = side_values(body, corners, g)
        out[0, at] = jnp.where(side < H, sides[0], own)
        out[1, at] = jnp.where(side < H, own, sides[1])

    def load_halos():
        ih[...] = jnp.zeros_like(ih)

        @pl.loop(0, levels)
        def _(l):
            for g in range(base + 1):
                t = g * levels + l
                halo = to_slot(jnp.concatenate([nm[t], prm[t]], axis=0), l)
                ih[g] = merge_slot(ih[g], halo, l)
                if g == base:
                    dx[l, rows:] = (0.5 * step_member) * halo
                else:
                    mx[g // fields, g % fields, l, rows:] = halo

        t = (base + 1) * levels
        halo = to_slot(jnp.concatenate([nm[t], prm[t]], axis=0), 0)
        rx[rows:] = step_member * halo
        ih[base + 1] = merge_slot(ih[base + 1], halo, 0)
        for g in range(base + 2):
            pack_strips(ym[g], ih[g], ym_in, mcor_in, g, strips, g)
        kappa = [(0.5 * step_member) * load(strips, s, base) for s in range(2)]
        khalo[...] = joined(kappa)
        for s in range(2):
            f = kappa[s]
            after, before = neighbours(f)
            edge_coef[s, 0] = f + up_x(f)
            edge_coef[s, 1] = f + after
            edge_coef[s, 2] = f + before
            spin = jnp.where(ids_m < SLOT, step_member * load(strips, s, base + 1), 0.0)
            width = SLOT
            while width < LANES:
                spin = spin + pltpu.roll(spin, width, 1)
                width *= 2
            edge_coef[s, 3] = spin
        for m in range(count):
            evolve_strips(strips, m * fields, m * fields + 1, m)

    def evolve(pairs, at, l):
        first = SLOT * l + H
        is_first, is_last = ids_m == first, ids_m == first - 1

        def beside(f, halo):
            after = pltpu.roll(jnp.where(is_first, halo, f), LANES - 1, 1)
            before = pltpu.roll(jnp.where(is_last, halo, f), 1, 1)
            return after, before

        kappa = load(dx, l)
        after, before = beside(kappa, khalo[...])
        east = kappa + up_x(kappa)
        north = kappa + after
        south = kappa + before
        spin = pltpu.roll(load(rx), SLOT * l, 1)
        out = []
        for (p, q), m in zip(pairs, at):
            for step in range(MSTEPS):
                moved = [
                    move(f, *beside(f, halos[m, step, k]), east, north, south)
                    for k, f in enumerate((p, q))
                ]
                p, q = moved[0] - spin * q, moved[1] + spin * p
            out += [pltpu.roll(f, LANES - first, 1) for f in (p, q)]
        return out

    def member_level(l):
        pairs = [[load(mx, m, f, l) for f in range(fields)] for m in range(count)]
        for k, value in enumerate(evolve(pairs, range(count), l)):
            store(mf_ref, value, k // fields, k % fields, l)

    def load_correction_halos():
        kih[...] = jnp.zeros_like(kih)

        @pl.loop(0, clevels)
        def _(l):
            for f in range(fields):
                t = f * clevels + l
                halo = to_slot(jnp.concatenate([ncorr[t], prcorr[t]], axis=0), me * clevels + l)
                kih[f] = merge_slot(kih[f], halo, me * clevels + l)
                kx[l, f, rows:] = halo

        for f in range(fields):
            pack_strips(ycorr[f], kih[f], ycorr_in, kcor_in, f, kstrips, f)
        evolve_strips(kstrips, 0, 1, count)

    def correction_level(l):
        pair = [load(kx, l, f) for f in range(fields)]
        for f, value in enumerate(evolve([pair], [count], me * clevels + l)):
            store(shift, value, l, f)

    landed(got_xm)
    landed(got_mc)
    load_halos()
    landed(got_sum)

    @pl.loop(0, clevels)
    def _(l):
        for f in range(fields):
            total = sums[me * clevels + l, f]
            for k in range(2 if square else n - 1):
                total = total + sums_in[k, l, f]
            tile = corr[l, f] - total * (1.0 / (count * n))
            rolled = to_slot(tile, me * clevels + l)
            kx[l, f, :rows] = rolled
            ycorr[f] = merge_slot(ycorr[f], rolled, me * clevels + l)
            hcorr[f * clevels + l] = tile[:H]
            tcorr[f * clevels + l] = tile[rows - H :]

    got_yk = send_y(ycorr, ycorr_in)
    got_xk = send_x(hcorr, tcorr, ncorr, prcorr)
    got_kc = send_corners(ycorr, kcor, kcor_in)

    cut_a = (4 * levels) // 16
    pl.loop(0, cut_a)(member_level)
    landed(got_yk)
    landed(got_xk)
    landed(got_kc)
    load_correction_halos()
    got_shift = []
    for l in range(clevels):
        correction_level(l)
        got_shift.append([
            send(shift.at[l], shift_in.at[k, l], target)
            for k, target in enumerate(near if square else peers)
        ])
    cut_b = cut_a
    if square:
        for l in range(clevels):
            cut_c = cut_a + (2 * levels * (l + 1)) // 16
            pl.loop(cut_b, cut_c)(member_level)
            cut_b = cut_c
            landed(got_shift[l])
            got_shift[l] = [
                send(shift_in.at[k, l, k], shift_in.at[2, l, k], near[1 - k]) for k in range(2)
            ]
    pl.loop(cut_b, levels)(member_level)

    def add(piece, at):
        for f in range(fields):
            tile = piece[f]
            for m in range(count):
                mf_ref[m, f, at] = mf_ref[m, f, at] + tile

    @pl.loop(0, clevels)
    def _(l):
        add(shift.at[l], me * clevels + l)

    ready = 2 if square else 0
    for k in range(ready):

        @pl.loop(0, clevels)
        def _(l):
            add(shift_in.at[k, l], owners[k] * clevels + l)

    for l in range(clevels):
        landed(got_shift[l])
        for k in range(ready, n - 1):
            add(shift_in.at[k, l], owners[k] * clevels + l)
    for copy in pending:
        copy.wait_send()
    assert len(pending) == copies


def per_device(control, members, diffusivity, rotation):
    fields, clevels, crows, ccols = control.shape
    count, _, levels, rows, cols = members.shape
    base = count * fields
    tiles = (base + 1) * levels + 1
    n = lax.axis_size("mem")
    ns = 2 if lax.axis_size("gy") > 2 else 1
    copies = 3 * (ns + 2 + 2 * ns) + (6 + 4 * clevels if n == 4 else (1 + clevels) * (n - 1))
    vmem = lambda *shape: pltpu.VMEM(shape, F32)
    height = rows + 2 * H
    scratch = (
        [vmem(fields * clevels, H, ccols)] * 4
        + [vmem(tiles, H, cols)] * 4
        + [vmem(1, crows, LANES), vmem(base + 2, rows, LANES)]
        + [vmem(ns, 1, crows, LANES), vmem(ns, base + 2, rows, LANES)]
        + [vmem(2, 1, H, LANES), vmem(2, base + 2, H, LANES)]
        + [vmem(ns, 2, 1, H, LANES), vmem(ns, 2, base + 2, H, LANES)]
        + [vmem(levels, fields, rows, cols), vmem(n - 1, clevels, fields, rows, cols)]
        + [vmem(clevels, fields, rows, cols)]
        + [vmem(fields * clevels, H, cols)] * 4
        + [vmem(fields, rows, LANES), vmem(ns, fields, rows, LANES)]
        + [vmem(2, fields, H, LANES), vmem(ns, 2, fields, H, LANES)]
        + [vmem(clevels, fields, rows, cols), vmem(n - 1, clevels, fields, rows, cols)]
        + [vmem(count, fields, levels, height, cols), vmem(levels, height, cols), vmem(height, cols)]
        + [vmem(clevels, fields, height, cols), vmem(base + 2, 2 * H, cols), vmem(fields, 2 * H, cols)]
        + [vmem(2, base + 2, height, cols), vmem(2, fields, height, cols), vmem(2, 4, height, cols)]
        + [vmem(count + 1, MSTEPS, fields, height, cols), vmem(height, cols)]
        + [vmem(clevels, fields, rows, cols)]
        + [pltpu.SemaphoreType.DMA((copies,))] * 2
    )
    return pl.pallas_call(
        functools.partial(fused_kernel, copies),
        in_specs=[pl.BlockSpec(memory_space=pltpu.VMEM)] * 4,
        out_specs=[pl.BlockSpec(memory_space=pltpu.VMEM)] * 2,
        out_shape=[
            jax.ShapeDtypeStruct(control.shape, F32),
            jax.ShapeDtypeStruct(members.shape, F32),
        ],
        scratch_shapes=scratch,
        compiler_params=pltpu.CompilerParams(collective_id=0, has_side_effects=True),
        name="fused",
    )(control, members, diffusivity, rotation)


def solution(mesh):
    in_specs = (
        P(None, "mem", "gx", "gy"),
        P("mem", None, None, "gx", "gy"),
        P(None, "gx", "gy"),
        P("gx", "gy"),
    )
    out_specs = (P(None, "mem", "gx", "gy"), P("mem", None, None, "gx", "gy"))
    return jax.shard_map(
        per_device, mesh=mesh, in_specs=in_specs, out_specs=out_specs, check_vma=False
    )
```

```python
import functools

import jax
import jax.numpy as jnp
from jax import lax
from jax.experimental import pallas as pl
from jax.experimental.pallas import tpu as pltpu
from jax.sharding import PartitionSpec as P

CSTEPS = 4
MSTEPS = 4
H = 4
SLOT = 2 * H
LANES = 128

step_control = 0.15
viscosity = 0.5
step_member = 0.5
F32 = jnp.float32


def lane_ids(rows):
    return lax.broadcasted_iota(jnp.int32, (rows, LANES), 1)


def to_slot(edges, slot):
    shift = H + SLOT * slot
    if not isinstance(slot, int):
        shift = lax.rem(shift, LANES)
    return pltpu.roll(edges, shift, 1)


def merge_slot(packed, rolled, slot):
    ids = lane_ids(rolled.shape[0])
    inside = (ids >= SLOT * slot) & (ids < SLOT * slot + SLOT)
    return jnp.where(inside, rolled, packed)


def put_slot(packed, edges, slot):
    return merge_slot(packed, to_slot(edges, slot), slot)


def side_block(left, right, slot):
    shift = lax.rem(2 * LANES - SLOT * slot - H, LANES)
    after = pltpu.roll(right, shift, 1)
    if left is right:
        return after
    before = pltpu.roll(left, shift, 1)
    return jnp.where(lane_ids(after.shape[0]) < LANES // 2, after, before)


def fused_kernel(
    copies, c_in, m_in, d_in, r_in, cf_ref, mf_ref, c_ref, m_ref, d_ref, r_ref,
    hc, tc, nc, prc, hm, tm, nm, prm, yc, ym, yc_in, ym_in, ccor, mcor, ccor_in, mcor_in,
    sums, sums_in, corr, hcorr, tcorr, ncorr, prcorr, ycorr, ycorr_in, kcor, kcor_in,
    shift, shift_in, mx, dx, rx, kx, ih, kih, strips, kstrips, edge_coef, halos, khalo, part,
    load_sem, send_sem, recv_sem,
):
    fields, clevels, crows, ccols = c_ref.shape
    count, _, levels, rows, cols = m_ref.shape
    base = count * fields
    nx, ny, n = lax.axis_size("gx"), lax.axis_size("gy"), lax.axis_size("mem")
    x, y, me = lax.axis_index("gx"), lax.axis_index("gy"), lax.axis_index("mem")
    two = ny > 2
    nsides = 2 if two else 1
    x_next, x_prev = {"gx": lax.rem(x + 1, nx)}, {"gx": lax.rem(x + nx - 1, nx)}
    y_next, y_prev = {"gy": lax.rem(y + 1, ny)}, {"gy": lax.rem(y + ny - 1, ny)}
    peers = [{"mem": lax.rem(me + k, n)} for k in range(1, n)]
    mesh_id = pl.DeviceIdType.MESH
    pending = []

    def send(src, dst, target):
        k = len(pending)
        copy = pltpu.make_async_remote_copy(
            src_ref=src, dst_ref=dst, send_sem=send_sem.at[k], recv_sem=recv_sem.at[k],
            device_id=target, device_id_type=mesh_id,
        )
        copy.start()
        pending.append(copy)
        return copy

    def landed(group):
        for copy in group:
            copy.wait_recv()

    def send_y(src, dst):
        group = [send(src, dst.at[0], y_next)]
        if two:
            group.append(send(src, dst.at[1], y_prev))
        return group

    def send_x(first, last, from_next, from_prev):
        return [send(first, from_next, x_prev), send(last, from_prev, x_next)]

    def send_corners(own, buf, buf_in):
        for g in range(own.shape[0]):
            tile = own[g]
            buf[0, g] = tile[:H]
            buf[1, g] = tile[tile.shape[0] - H :]
        group = []
        for k, across in enumerate([y_next] + ([y_prev] if two else [])):
            group.append(send(buf.at[0], buf_in.at[k, 0], {**x_prev, **across}))
            group.append(send(buf.at[1], buf_in.at[k, 1], {**x_next, **across}))
        return group

    barrier = pltpu.get_barrier_semaphore()
    greeted = [x_next, x_prev, y_next] + ([y_prev] if two else []) + peers
    for across in [y_next] + ([y_prev] if two else []):
        greeted += [{**x_next, **across}, {**x_prev, **across}]
    for target in greeted:
        pl.semaphore_signal(barrier, inc=1, device_id=target, device_id_type=mesh_id)

    loads = [
        pltpu.make_async_copy(src, dst, load_sem.at[k])
        for k, (src, dst) in enumerate(
            [(c_in, c_ref), (m_in, m_ref), (d_in, d_ref), (r_in, r_ref)]
        )
    ]
    for copy in loads:
        copy.start()

    ids = lane_ids(crows)
    yc[...] = jnp.zeros_like(yc)
    ym[...] = jnp.zeros_like(ym)
    ycorr[...] = jnp.zeros_like(ycorr)
    loads[0].wait()

    @pl.loop(0, clevels)
    def _(l):
        for f in range(fields):
            first = c_ref[f, l, :, :LANES]
            last = c_ref[f, l, :, ccols - LANES :]
            t = f * clevels + l
            yc[0] = put_slot(yc[0], jnp.where(ids < LANES // 2, first, last), t)
            hc[t] = c_ref[f, l, :H]
            tc[t] = c_ref[f, l, crows - H :]

    loads[1].wait()

    @pl.loop(0, levels)
    def _(l):
        for f in range(fields):
            total = m_ref[0, f, l]
            for m in range(1, count):
                total = total + m_ref[m, f, l]
            sums[l, f] = total

    pl.semaphore_wait(barrier, len(greeted))
    got_yc = send_y(yc, yc_in)
    got_xc = send_x(hc, tc, nc, prc)
    got_cc = send_corners(yc, ccor, ccor_in)
    square = n == 4

    def piece(owner, *f):
        return sums.at[(pl.ds(owner * clevels, clevels), *f)]

    if square:
        owners = [me + 1 - 2 * lax.rem(me, 2), me + 2 - 4 * (me // 2), 3 - me]
        near = [{"mem": owners[0]}, {"mem": owners[1]}]
        got_far = [send(piece(owners[2], k), sums_in.at[2, :, k], near[k]) for k in range(2)]
        got_sum = [send(piece(owners[k], k), sums_in.at[k, :, k], near[k]) for k in range(2)]
    else:
        owners = [lax.rem(me + n - 1 - k, n) for k in range(n - 1)]
        got_sum = [
            send(piece(lax.rem(me + k, n)), sums_in.at[k - 1], peers[k - 1]) for k in range(1, n)
        ]

    for copy in loads[2:]:
        copy.wait()

    @pl.loop(0, levels)
    def _(l):
        for f in range(fields):
            for m in range(count):
                tile = m_ref[m, f, l]
                g = m * fields + f
                rolled = to_slot(tile, l)
                mx[m, f, l, :rows] = rolled
                ym[g] = merge_slot(ym[g], rolled, l)
                hm[g * levels + l] = tile[:H]
                tm[g * levels + l] = tile[rows - H :]
        tile = d_ref[l]
        rolled = to_slot(tile, l)
        dx[l, :rows] = (0.5 * step_member) * rolled
        ym[base] = merge_slot(ym[base], rolled, l)
        hm[base * levels + l] = tile[:H]
        tm[base * levels + l] = tile[rows - H :]

    tile = r_ref[...]
    rolled = to_slot(tile, 0)
    rx[:rows] = step_member * rolled
    ym[base + 1] = merge_slot(jnp.zeros((rows, LANES), F32), rolled, 0)
    hm[(base + 1) * levels] = tile[:H]
    tm[(base + 1) * levels] = tile[rows - H :]
    got_ym = send_y(ym, ym_in)
    got_xm = send_x(hm, tm, nm, prm)
    got_mc = send_corners(ym, mcor, mcor_in)
    landed(got_yc)
    landed(got_xc)
    landed(got_cc)
    if square:
        for k in range(2):
            landed([got_far[k]])

            @pl.loop(0, clevels)
            def _(l):
                part[l, k] = sums[owners[1 - k] * clevels + l, k] + sums_in[2, l, k]

            got_sum.append(send(part.at[:, k], sums_in.at[1 - k, :, k], near[1 - k]))

    def side_values(body, corners, g):
        out = [
            jnp.concatenate([body[s, g], corners[s, 0, g], corners[s, 1, g]], axis=0)
            for s in range(nsides)
        ]
        return out[0], out[-1]

    half_x, half_y = crows // 2, ccols // 2
    height, full = crows + 2 * H, ccols + LANES

    def control_level(l):
        left, right = side_values(yc_in, ccor_in, 0)
        body = []
        for f in range(fields):
            t = f * clevels + l
            own = jnp.concatenate([c_ref[f, l], nc[t], prc[t]], axis=0)
            body.append(jnp.concatenate([own, side_block(left, right, t)], axis=1))
        for _ in range(CSTEPS):
            a = body[0] * (0.5 * step_control)
            b = body[1] * (0.5 * step_control)
            new = []
            for f in body:
                ux = pltpu.roll(f, height - 1, 0)
                lx = pltpu.roll(f, 1, 0)
                uy = pltpu.roll(f, full - 1, 1)
                ly = pltpu.roll(f, 1, 1)
                lap = (ux + lx) + (uy + ly) - 4.0 * f
                new.append(f + ((step_control * viscosity) * lap - a * (ux - lx) - b * (uy - ly)))
            body = new
        pick_y = (
            lax.broadcasted_iota(jnp.int32, (ccols, half_y), 0) // 2
            == lax.broadcasted_iota(jnp.int32, (ccols, half_y), 1)
        ).astype(F32)
        pick_x = (
            lax.broadcasted_iota(jnp.int32, (half_x, crows), 1) // 2
            == lax.broadcasted_iota(jnp.int32, (half_x, crows), 0)
        ).astype(F32)
        for f in range(fields):
            field = body[f][:crows, :ccols]
            cf_ref[f, l] = field
            t = jnp.dot(field, pick_y, precision=lax.Precision.HIGHEST, preferred_element_type=F32)
            t = jnp.dot(pick_x, t, precision=lax.Precision.HIGHEST, preferred_element_type=F32)
            corr[l, f] = 0.25 * t

    pl.loop(0, clevels)(control_level)
    landed(got_ym)
    height = rows + 2 * H
    stride = height // 8
    side = lax.rem(lane_ids(height), SLOT)

    def load(ref, *at):
        return jnp.concatenate(
            [ref[(*at, pl.ds(i, 8, stride=stride), slice(None))] for i in range(stride)], axis=0
        )

    def store(ref, value, *at):
        for i in range(stride):
            kept = (rows - i + stride - 1) // stride
            ref[(*at, pl.ds(i, kept, stride=stride), slice(None))] = value[8 * i : 8 * i + kept]

    def up_x(f):
        return jnp.concatenate([f[8:], pltpu.roll(f[:8], 7, 0)], axis=0)

    def low_x(f):
        return jnp.concatenate([pltpu.roll(f[-8:], 1, 0), f[:-8]], axis=0)

    ids_m = lane_ids(height)

    def move(f, after, before, east, north, south):
        fx = east * (up_x(f) - f)
        return (f + north * (after - f)) + (south * (before - f) + (fx - low_x(fx)))

    def neighbours(f):
        return pltpu.roll(f, LANES - 1, 1), pltpu.roll(f, 1, 1)

    def joined(pair):
        return jnp.where(side == H - 1, pair[0], pair[1])

    def evolve_strips(ref, p_at, q_at, at):
        now = [[load(ref, s, g) for s in range(2)] for g in (p_at, q_at)]
        for step in range(MSTEPS):
            for f in range(2):
                halos[at, step, f] = joined(now[f])
            if step == MSTEPS - 1:
                break
            new = [[], []]
            for s in range(2):
                w = [edge_coef[s, k] for k in range(4)]
                p, q = [move(f[s], *neighbours(f[s]), *w[:3]) for f in now]
                new[0].append(p - w[3] * now[1][s])
                new[1].append(q + w[3] * now[0][s])
            now = new

    def pack_strips(own, halo, body, corners, g, out, at):
        own = jnp.concatenate([own, halo], axis=0)
        sides = side_values(body, corners, g)
        out[0, at] = jnp.where(side < H, sides[0], own)
        out[1, at] = jnp.where(side < H, own, sides[1])

    def load_halos():
        ih[...] = jnp.zeros_like(ih)

        @pl.loop(0, levels)
        def _(l):
            for g in range(base + 1):
                t = g * levels + l
                halo = to_slot(jnp.concatenate([nm[t], prm[t]], axis=0), l)
                ih[g] = merge_slot(ih[g], halo, l)
                if g == base:
                    dx[l, rows:] = (0.5 * step_member) * halo
                else:
                    mx[g // fields, g % fields, l, rows:] = halo

        t = (base + 1) * levels
        halo = to_slot(jnp.concatenate([nm[t], prm[t]], axis=0), 0)
        rx[rows:] = step_member * halo
        ih[base + 1] = merge_slot(ih[base + 1], halo, 0)
        for g in range(base + 2):
            pack_strips(ym[g], ih[g], ym_in, mcor_in, g, strips, g)
        kappa = [(0.5 * step_member) * load(strips, s, base) for s in range(2)]
        khalo[...] = joined(kappa)
        for s in range(2):
            f = kappa[s]
            after, before = neighbours(f)
            edge_coef[s, 0] = f + up_x(f)
            edge_coef[s, 1] = f + after
            edge_coef[s, 2] = f + before
            spin = jnp.where(ids_m < SLOT, step_member * load(strips, s, base + 1), 0.0)
            width = SLOT
            while width < LANES:
                spin = spin + pltpu.roll(spin, width, 1)
                width *= 2
            edge_coef[s, 3] = spin
        for m in range(count):
            evolve_strips(strips, m * fields, m * fields + 1, m)

    def evolve(pairs, at, l):
        first = SLOT * l + H
        is_first, is_last = ids_m == first, ids_m == first - 1

        def beside(f, halo):
            after = pltpu.roll(jnp.where(is_first, halo, f), LANES - 1, 1)
            before = pltpu.roll(jnp.where(is_last, halo, f), 1, 1)
            return after, before

        kappa = load(dx, l)
        after, before = beside(kappa, khalo[...])
        east = kappa + up_x(kappa)
        north = kappa + after
        south = kappa + before
        spin = pltpu.roll(load(rx), SLOT * l, 1)
        out = []
        for (p, q), m in zip(pairs, at):
            for step in range(MSTEPS):
                moved = [
                    move(f, *beside(f, halos[m, step, k]), east, north, south)
                    for k, f in enumerate((p, q))
                ]
                p, q = moved[0] - spin * q, moved[1] + spin * p
            out += [pltpu.roll(f, LANES - first, 1) for f in (p, q)]
        return out

    def member_level(l):
        pairs = [[load(mx, m, f, l) for f in range(fields)] for m in range(count)]
        for k, value in enumerate(evolve(pairs, range(count), l)):
            store(mf_ref, value, k // fields, k % fields, l)

    def load_correction_halos():
        kih[...] = jnp.zeros_like(kih)

        @pl.loop(0, clevels)
        def _(l):
            for f in range(fields):
                t = f * clevels + l
                halo = to_slot(jnp.concatenate([ncorr[t], prcorr[t]], axis=0), me * clevels + l)
                kih[f] = merge_slot(kih[f], halo, me * clevels + l)
                kx[l, f, rows:] = halo

        for f in range(fields):
            pack_strips(ycorr[f], kih[f], ycorr_in, kcor_in, f, kstrips, f)
        evolve_strips(kstrips, 0, 1, count)

    def correction_level(l):
        pair = [load(kx, l, f) for f in range(fields)]
        for f, value in enumerate(evolve([pair], [count], me * clevels + l)):
            store(shift, value, l, f)

    landed(got_sum)

    @pl.loop(0, clevels)
    def _(l):
        for f in range(fields):
            total = sums[me * clevels + l, f]
            for k in range(2 if square else n - 1):
                total = total + sums_in[k, l, f]
            tile = corr[l, f] - total * (1.0 / (count * n))
            rolled = to_slot(tile, me * clevels + l)
            kx[l, f, :rows] = rolled
            ycorr[f] = merge_slot(ycorr[f], rolled, me * clevels + l)
            hcorr[f * clevels + l] = tile[:H]
            tcorr[f * clevels + l] = tile[rows - H :]

    got_yk = send_y(ycorr, ycorr_in)
    got_xk = send_x(hcorr, tcorr, ncorr, prcorr)
    got_kc = send_corners(ycorr, kcor, kcor_in)

    landed(got_xm)
    landed(got_mc)
    load_halos()
    cut_a = (4 * levels) // 16
    pl.loop(0, cut_a)(member_level)
    landed(got_yk)
    landed(got_xk)
    landed(got_kc)
    load_correction_halos()
    got_shift = []
    for l in range(clevels):
        correction_level(l)
        got_shift.append([
            send(shift.at[l], shift_in.at[k, l], target)
            for k, target in enumerate(near if square else peers)
        ])
    cut_b = cut_a
    if square:
        for l in range(clevels):
            cut_c = cut_a + (2 * levels * (l + 1)) // 16
            pl.loop(cut_b, cut_c)(member_level)
            cut_b = cut_c
            landed(got_shift[l])
            got_shift[l] = [
                send(shift_in.at[k, l, k], shift_in.at[2, l, k], near[1 - k]) for k in range(2)
            ]
    pl.loop(cut_b, levels)(member_level)

    def add(piece, at):
        for f in range(fields):
            tile = piece[f]
            for m in range(count):
                mf_ref[m, f, at] = mf_ref[m, f, at] + tile

    @pl.loop(0, clevels)
    def _(l):
        add(shift.at[l], me * clevels + l)

    ready = 2 if square else 0
    for k in range(ready):

        @pl.loop(0, clevels)
        def _(l):
            add(shift_in.at[k, l], owners[k] * clevels + l)

    for l in range(clevels):
        landed(got_shift[l])
        for k in range(ready, n - 1):
            add(shift_in.at[k, l], owners[k] * clevels + l)
    for copy in pending:
        copy.wait_send()
    assert len(pending) == copies


def write_kernel(c_ref, m_ref, c_out, m_out, sem):
    group = [
        pltpu.make_async_copy(src, dst, sem.at[k])
        for k, (src, dst) in enumerate([(m_ref, m_out), (c_ref, c_out)])
    ]
    for copy in group:
        copy.start()
    for copy in group:
        copy.wait()


def per_device(control, members, diffusivity, rotation):
    fields, clevels, crows, ccols = control.shape
    count, _, levels, rows, cols = members.shape
    base = count * fields
    tiles = (base + 1) * levels + 1
    n = lax.axis_size("mem")
    ns = 2 if lax.axis_size("gy") > 2 else 1
    copies = 3 * (ns + 2 + 2 * ns) + (6 + 4 * clevels if n == 4 else (1 + clevels) * (n - 1))
    vmem = lambda *shape: pltpu.VMEM(shape, F32)
    height = rows + 2 * H
    scratch = (
        [vmem(*a.shape) for a in (control, members, diffusivity, rotation)]
        + [vmem(fields * clevels, H, ccols)] * 4
        + [vmem(tiles, H, cols)] * 4
        + [vmem(1, crows, LANES), vmem(base + 2, rows, LANES)]
        + [vmem(ns, 1, crows, LANES), vmem(ns, base + 2, rows, LANES)]
        + [vmem(2, 1, H, LANES), vmem(2, base + 2, H, LANES)]
        + [vmem(ns, 2, 1, H, LANES), vmem(ns, 2, base + 2, H, LANES)]
        + [vmem(levels, fields, rows, cols), vmem(n - 1, clevels, fields, rows, cols)]
        + [vmem(clevels, fields, rows, cols)]
        + [vmem(fields * clevels, H, cols)] * 4
        + [vmem(fields, rows, LANES), vmem(ns, fields, rows, LANES)]
        + [vmem(2, fields, H, LANES), vmem(ns, 2, fields, H, LANES)]
        + [vmem(clevels, fields, rows, cols), vmem(n - 1, clevels, fields, rows, cols)]
        + [vmem(count, fields, levels, height, cols), vmem(levels, height, cols), vmem(height, cols)]
        + [vmem(clevels, fields, height, cols), vmem(base + 2, 2 * H, cols), vmem(fields, 2 * H, cols)]
        + [vmem(2, base + 2, height, cols), vmem(2, fields, height, cols), vmem(2, 4, height, cols)]
        + [vmem(count + 1, MSTEPS, fields, height, cols), vmem(height, cols)]
        + [vmem(clevels, fields, rows, cols)]
        + [pltpu.SemaphoreType.DMA((4,))] + [pltpu.SemaphoreType.DMA((copies,))] * 2
    )
    space = lambda m, k: [pl.BlockSpec(memory_space=m)] * k
    held = pl.pallas_call(
        functools.partial(fused_kernel, copies),
        in_specs=space(pl.ANY, 4),
        out_specs=space(pltpu.VMEM, 2),
        out_shape=[pltpu.VMEM(control.shape, F32), pltpu.VMEM(members.shape, F32)],
        scratch_shapes=scratch,
        compiler_params=pltpu.CompilerParams(
            collective_id=0, has_side_effects=True, vmem_limit_bytes=121 * 2**19
        ),
        name="fused",
    )(control, members, diffusivity, rotation)
    return pl.pallas_call(
        write_kernel,
        in_specs=space(pl.ANY, 2),
        out_specs=space(pl.ANY, 2),
        out_shape=[jax.ShapeDtypeStruct(a.shape, F32) for a in (control, members)],
        scratch_shapes=[pltpu.SemaphoreType.DMA((2,))],
        compiler_params=pltpu.CompilerParams(vmem_limit_bytes=2**20),
        name="write",
    )(*held)


def solution(mesh):
    in_specs = (
        P(None, "mem", "gx", "gy"),
        P("mem", None, None, "gx", "gy"),
        P(None, "gx", "gy"),
        P("gx", "gy"),
    )
    out_specs = (P(None, "mem", "gx", "gy"), P("mem", None, None, "gx", "gy"))
    return jax.shard_map(
        per_device, mesh=mesh, in_specs=in_specs, out_specs=out_specs, check_vma=False
    )
```

```python
import functools

import jax
import jax.numpy as jnp
from jax import lax
from jax.experimental import pallas as pl
from jax.experimental.pallas import tpu as pltpu
from jax.sharding import PartitionSpec as P

CSTEPS = 4
MSTEPS = 4
H = 4
SLOT = 2 * H
LANES = 128

step_control = 0.15
viscosity = 0.5
step_member = 0.5
F32 = jnp.float32


def lane_ids(rows):
    return lax.broadcasted_iota(jnp.int32, (rows, LANES), 1)


def to_slot(edges, slot):
    shift = H + SLOT * slot
    if not isinstance(slot, int):
        shift = lax.rem(shift, LANES)
    return pltpu.roll(edges, shift, 1)


def merge_slot(packed, rolled, slot):
    ids = lane_ids(rolled.shape[0])
    inside = (ids >= SLOT * slot) & (ids < SLOT * slot + SLOT)
    return jnp.where(inside, rolled, packed)


def put_slot(packed, edges, slot):
    return merge_slot(packed, to_slot(edges, slot), slot)


def side_block(left, right, slot):
    shift = lax.rem(2 * LANES - SLOT * slot - H, LANES)
    after = pltpu.roll(right, shift, 1)
    if left is right:
        return after
    before = pltpu.roll(left, shift, 1)
    return jnp.where(lane_ids(after.shape[0]) < LANES // 2, after, before)


def fused_kernel(
    copies, c_in, m_in, d_in, r_in, cf_ref, mf_ref, c_ref, m_ref, d_ref, r_ref,
    hc, tc, nc, prc, hm, tm, nm, prm, yc, ym, yc_in, ym_in, ccor, mcor, ccor_in, mcor_in,
    sums, sums_in, corr, hcorr, tcorr, ncorr, prcorr, ycorr, ycorr_in, kcor, kcor_in,
    shift, shift_in, mx, dx, rx, kx, ih, kih, strips, kstrips, edge_coef, halos, khalo, part,
    cih, cstrips, chalos, pairs_of, pick,
    load_sem, send_sem, recv_sem,
):
    fields, clevels, wide, cheight, _ = c_ref.shape
    crows, ccols = cheight - 2 * H, wide * LANES
    columns = [slice(c * LANES, (c + 1) * LANES) for c in range(wide)]
    count, _, levels, rows, cols = m_ref.shape
    base = count * fields
    nx, ny, n = lax.axis_size("gx"), lax.axis_size("gy"), lax.axis_size("mem")
    x, y, me = lax.axis_index("gx"), lax.axis_index("gy"), lax.axis_index("mem")
    two = ny > 2
    nsides = 2 if two else 1
    x_next, x_prev = {"gx": lax.rem(x + 1, nx)}, {"gx": lax.rem(x + nx - 1, nx)}
    y_next, y_prev = {"gy": lax.rem(y + 1, ny)}, {"gy": lax.rem(y + ny - 1, ny)}
    peers = [{"mem": lax.rem(me + k, n)} for k in range(1, n)]
    mesh_id = pl.DeviceIdType.MESH
    pending = []

    def send(src, dst, target):
        k = len(pending)
        copy = pltpu.make_async_remote_copy(
            src_ref=src, dst_ref=dst, send_sem=send_sem.at[k], recv_sem=recv_sem.at[k],
            device_id=target, device_id_type=mesh_id,
        )
        copy.start()
        pending.append(copy)
        return copy

    def landed(group):
        for copy in group:
            copy.wait_recv()

    def send_y(src, dst):
        group = [send(src, dst.at[0], y_next)]
        if two:
            group.append(send(src, dst.at[1], y_prev))
        return group

    def send_x(first, last, from_next, from_prev):
        return [send(first, from_next, x_prev), send(last, from_prev, x_next)]

    def send_corners(own, buf, buf_in):
        for g in range(own.shape[0]):
            tile = own[g]
            buf[0, g] = tile[:H]
            buf[1, g] = tile[tile.shape[0] - H :]
        group = []
        for k, across in enumerate([y_next] + ([y_prev] if two else [])):
            group.append(send(buf.at[0], buf_in.at[k, 0], {**x_prev, **across}))
            group.append(send(buf.at[1], buf_in.at[k, 1], {**x_next, **across}))
        return group

    barrier = pltpu.get_barrier_semaphore()
    greeted = [x_next, x_prev, y_next] + ([y_prev] if two else []) + peers
    for across in [y_next] + ([y_prev] if two else []):
        greeted += [{**x_next, **across}, {**x_prev, **across}]
    for target in greeted:
        pl.semaphore_signal(barrier, inc=1, device_id=target, device_id_type=mesh_id)

    loads = [
        pltpu.make_async_copy(src, dst, load_sem.at[k])
        for k, (src, dst) in enumerate(
            [
                (c_in.at[:, :, :, pl.ds(c * LANES, LANES)], c_ref.at[:, :, c, pl.ds(0, crows), :])
                for c in range(wide)
            ]
            + [(m_in, m_ref), (d_in, d_ref), (r_in, r_ref)]
        )
    ]
    for copy in loads:
        copy.start()

    ids = lane_ids(crows)
    yc[...] = jnp.zeros_like(yc)
    ym[...] = jnp.zeros_like(ym)
    ycorr[...] = jnp.zeros_like(ycorr)
    for copy in loads[:wide]:
        copy.wait()

    @pl.loop(0, clevels)
    def _(l):
        for f in range(fields):
            first = c_ref[f, l, 0, :crows]
            last = c_ref[f, l, wide - 1, :crows]
            t = f * clevels + l
            yc[0] = put_slot(yc[0], jnp.where(ids < LANES // 2, first, last), t)
            for c, column in enumerate(columns):
                hc[t, :, column] = c_ref[f, l, c, :H]
                tc[t, :, column] = c_ref[f, l, c, crows - H : crows]

    loads[wide].wait()

    @pl.loop(0, levels)
    def _(l):
        for f in range(fields):
            total = m_ref[0, f, l]
            for m in range(1, count):
                total = total + m_ref[m, f, l]
            sums[l, f] = total

    pl.semaphore_wait(barrier, len(greeted))
    got_yc = send_y(yc, yc_in)
    got_xc = send_x(hc, tc, nc, prc)
    got_cc = send_corners(yc, ccor, ccor_in)
    square = n == 4

    def piece(owner, *f):
        return sums.at[(pl.ds(owner * clevels, clevels), *f)]

    if square:
        owners = [me + 1 - 2 * lax.rem(me, 2), me + 2 - 4 * (me // 2), 3 - me]
        near = [{"mem": owners[0]}, {"mem": owners[1]}]
        got_far = [send(piece(owners[2], k), sums_in.at[2, :, k], near[k]) for k in range(2)]
        got_sum = [send(piece(owners[k], k), sums_in.at[k, :, k], near[k]) for k in range(2)]
    else:
        owners = [lax.rem(me + n - 1 - k, n) for k in range(n - 1)]
        got_sum = [
            send(piece(lax.rem(me + k, n)), sums_in.at[k - 1], peers[k - 1]) for k in range(1, n)
        ]

    for copy in loads[wide + 1 :]:
        copy.wait()

    @pl.loop(0, levels)
    def _(l):
        for f in range(fields):
            for m in range(count):
                tile = m_ref[m, f, l]
                g = m * fields + f
                rolled = to_slot(tile, l)
                mx[m, f, l, :rows] = rolled
                ym[g] = merge_slot(ym[g], rolled, l)
                hm[g * levels + l] = tile[:H]
                tm[g * levels + l] = tile[rows - H :]
        tile = d_ref[l]
        rolled = to_slot(tile, l)
        dx[l, :rows] = (0.5 * step_member) * rolled
        ym[base] = merge_slot(ym[base], rolled, l)
        hm[base * levels + l] = tile[:H]
        tm[base * levels + l] = tile[rows - H :]

    tile = r_ref[...]
    rolled = to_slot(tile, 0)
    rx[:rows] = step_member * rolled
    ym[base + 1] = merge_slot(jnp.zeros((rows, LANES), F32), rolled, 0)
    hm[(base + 1) * levels] = tile[:H]
    tm[(base + 1) * levels] = tile[rows - H :]
    got_ym = send_y(ym, ym_in)
    got_xm = send_x(hm, tm, nm, prm)
    got_mc = send_corners(ym, mcor, mcor_in)
    landed(got_yc)
    landed(got_xc)
    landed(got_cc)
    if square:
        for k in range(2):
            landed([got_far[k]])

            @pl.loop(0, clevels)
            def _(l):
                part[l, k] = sums[owners[1 - k] * clevels + l, k] + sums_in[2, l, k]

            got_sum.append(send(part.at[:, k], sums_in.at[1 - k, :, k], near[1 - k]))

    def side_values(body, corners, g):
        out = [
            jnp.concatenate([body[s, g], corners[s, 0, g], corners[s, 1, g]], axis=0)
            for s in range(nsides)
        ]
        return out[0], out[-1]

    height = rows + 2 * H
    side = lax.rem(lane_ids(height), SLOT)

    def load(ref, *at):
        stride = ref.shape[len(at)] // 8
        return jnp.concatenate(
            [ref[(*at, pl.ds(i, 8, stride=stride), slice(None))] for i in range(stride)], axis=0
        )

    def store(ref, value, *at):
        stride, kept = value.shape[0] // 8, ref.shape[len(at)]
        for i in range(stride):
            number = (kept - i + stride - 1) // stride
            ref[(*at, pl.ds(i, number, stride=stride), slice(None))] = value[8 * i : 8 * i + number]

    def up_x(f):
        return jnp.concatenate([f[8:], pltpu.roll(f[:8], 7, 0)], axis=0)

    def low_x(f):
        return jnp.concatenate([pltpu.roll(f[-8:], 1, 0), f[:-8]], axis=0)

    def neighbours(f):
        return pltpu.roll(f, LANES - 1, 1), pltpu.roll(f, 1, 1)

    half_x, half_y = crows // 2, ccols // 2
    cids = lane_ids(cheight)
    cside = lax.rem(cids, SLOT)
    pick[...] = jnp.where(
        lax.broadcasted_iota(jnp.int32, (ccols, half_y), 0) // 2
        == lax.broadcasted_iota(jnp.int32, (ccols, half_y), 1),
        0.25,
        0.0,
    )

    def joined(pair):
        ids = cside[: pair[0].shape[0]]
        return jnp.where(ids == H - 1, pair[0], pair[1])

    def burgers(f, after, before, u, v):
        total = (1.0 - u) * up_x(f) + (1.0 + u) * low_x(f)
        total = total + ((1.0 - v) * after + (1.0 + v) * before)
        diffusion = step_control * viscosity
        return (1.0 - 4.0 * diffusion) * f + diffusion * total

    def load_control_halos():
        cih[...] = jnp.zeros_like(cih)

        @pl.loop(0, clevels)
        def _(l):
            for f in range(fields):
                t = f * clevels + l
                ends = [
                    jnp.concatenate([nc[t, :, column], prc[t, :, column]], axis=0)
                    for column in columns
                ]
                for c in range(wide):
                    c_ref[f, l, c, crows:] = ends[c]
                edge = jnp.where(lane_ids(2 * H) < LANES // 2, ends[0], ends[-1])
                cih[...] = put_slot(cih[...], edge, t)

        own = jnp.concatenate([yc[0], cih[...]], axis=0)
        sides = side_values(yc_in, ccor_in, 0)
        cstrips[0] = jnp.where(cside < H, sides[0], own)
        cstrips[1] = jnp.where(cside < H, own, sides[1])
        first = [load(cstrips, s) for s in range(2)]
        now = [first, [pltpu.roll(f, LANES - SLOT * clevels, 1) for f in first]]
        for step in range(CSTEPS):
            for f in range(fields):
                chalos[step, f] = joined(now[f])
            if step < CSTEPS - 1:
                now = [
                    [burgers(f[s], *neighbours(f[s]), now[0][s], now[1][s]) for s in range(2)]
                    for f in now
                ]

    def control_level(l):
        body = [[load(c_ref, f, l, c) for c in range(wide)] for f in range(fields)]
        for step in range(CSTEPS):
            new = []
            for f, field in enumerate(body):
                halo = pltpu.roll(chalos[step, f], LANES - H - SLOT * l, 1)
                row = []
                for c in range(wide):
                    right = field[c + 1] if c + 1 < wide else halo
                    left = field[c - 1] if c else halo
                    after = pltpu.roll(jnp.where(cids == 0, right, field[c]), LANES - 1, 1)
                    before = pltpu.roll(jnp.where(cids == LANES - 1, left, field[c]), 1, 1)
                    row.append(burgers(field[c], after, before, body[0][c], body[1][c]))
                new.append(row)
            body = new
        for f in range(fields):
            for c in range(wide):
                store(cf_ref, body[f][c], f, l, c)
                store(pairs_of, body[f][c] + up_x(body[f][c]), f, c)
        even = [
            jnp.concatenate(
                [pairs_of[f, c, pl.ds(0, half_x, stride=2), :] for c in range(wide)], axis=1
            )
            for f in range(fields)
        ]
        small = jnp.dot(
            jnp.concatenate(even, axis=0), pick[...],
            precision=lax.Precision.HIGHEST, preferred_element_type=F32,
        )
        for f in range(fields):
            corr[l, f] = small[f * half_x : (f + 1) * half_x]

    load_control_halos()
    pl.loop(0, clevels)(control_level)
    landed(got_ym)
    ids_m = lane_ids(height)

    def move(f, after, before, east, north, south):
        fx = east * (up_x(f) - f)
        return (f + north * (after - f)) + (south * (before - f) + (fx - low_x(fx)))

    def evolve_strips(ref, p_at, q_at, at):
        now = [[load(ref, s, g) for s in range(2)] for g in (p_at, q_at)]
        for step in range(MSTEPS):
            for f in range(2):
                halos[at, step, f] = joined(now[f])
            if step == MSTEPS - 1:
                break
            new = [[], []]
            for s in range(2):
                w = [edge_coef[s, k] for k in range(4)]
                p, q = [move(f[s], *neighbours(f[s]), *w[:3]) for f in now]
                new[0].append(p - w[3] * now[1][s])
                new[1].append(q + w[3] * now[0][s])
            now = new

    def pack_strips(own, halo, body, corners, g, out, at):
        own = jnp.concatenate([own, halo], axis=0)
        sides = side_values(body, corners, g)
        out[0, at] = jnp.where(side < H, sides[0], own)
        out[1, at] = jnp.where(side < H, own, sides[1])

    def load_halos():
        ih[...] = jnp.zeros_like(ih)

        @pl.loop(0, levels)
        def _(l):
            for g in range(base + 1):
                t = g * levels + l
                halo = to_slot(jnp.concatenate([nm[t], prm[t]], axis=0), l)
                ih[g] = merge_slot(ih[g], halo, l)
                if g == base:
                    dx[l, rows:] = (0.5 * step_member) * halo
                else:
                    mx[g // fields, g % fields, l, rows:] = halo

        t = (base + 1) * levels
        halo = to_slot(jnp.concatenate([nm[t], prm[t]], axis=0), 0)
        rx[rows:] = step_member * halo
        ih[base + 1] = merge_slot(ih[base + 1], halo, 0)
        for g in range(base + 2):
            pack_strips(ym[g], ih[g], ym_in, mcor_in, g, strips, g)
        kappa = [(0.5 * step_member) * load(strips, s, base) for s in range(2)]
        khalo[...] = joined(kappa)
        for s in range(2):
            f = kappa[s]
            after, before = neighbours(f)
            edge_coef[s, 0] = f + up_x(f)
            edge_coef[s, 1] = f + after
            edge_coef[s, 2] = f + before
            spin = jnp.where(ids_m < SLOT, step_member * load(strips, s, base + 1), 0.0)
            width = SLOT
            while width < LANES:
                spin = spin + pltpu.roll(spin, width, 1)
                width *= 2
            edge_coef[s, 3] = spin
        for m in range(count):
            evolve_strips(strips, m * fields, m * fields + 1, m)

    def evolve(pairs, at, l):
        first = SLOT * l + H
        is_first, is_last = ids_m == first, ids_m == first - 1

        def beside(f, halo):
            after = pltpu.roll(jnp.where(is_first, halo, f), LANES - 1, 1)
            before = pltpu.roll(jnp.where(is_last, halo, f), 1, 1)
            return after, before

        kappa = load(dx, l)
        after, before = beside(kappa, khalo[...])
        east = kappa + up_x(kappa)
        north = kappa + after
        south = kappa + before
        spin = pltpu.roll(load(rx), SLOT * l, 1)
        out = []
        for (p, q), m in zip(pairs, at):
            for step in range(MSTEPS):
                moved = [
                    move(f, *beside(f, halos[m, step, k]), east, north, south)
                    for k, f in enumerate((p, q))
                ]
                p, q = moved[0] - spin * q, moved[1] + spin * p
            out += [pltpu.roll(f, LANES - first, 1) for f in (p, q)]
        return out

    def member_level(l):
        pairs = [[load(mx, m, f, l) for f in range(fields)] for m in range(count)]
        for k, value in enumerate(evolve(pairs, range(count), l)):
            store(mf_ref, value, k // fields, k % fields, l)

    def load_correction_halos():
        kih[...] = jnp.zeros_like(kih)

        @pl.loop(0, clevels)
        def _(l):
            for f in range(fields):
                t = f * clevels + l
                halo = to_slot(jnp.concatenate([ncorr[t], prcorr[t]], axis=0), me * clevels + l)
                kih[f] = merge_slot(kih[f], halo, me * clevels + l)
                kx[l, f, rows:] = halo

        for f in range(fields):
            pack_strips(ycorr[f], kih[f], ycorr_in, kcor_in, f, kstrips, f)
        evolve_strips(kstrips, 0, 1, count)

    def correction_level(l):
        pair = [load(kx, l, f) for f in range(fields)]
        for f, value in enumerate(evolve([pair], [count], me * clevels + l)):
            store(shift, value, l, f)

    landed(got_sum)

    @pl.loop(0, clevels)
    def _(l):
        for f in range(fields):
            total = sums[me * clevels + l, f]
            for k in range(2 if square else n - 1):
                total = total + sums_in[k, l, f]
            tile = corr[l, f] - total * (1.0 / (count * n))
            rolled = to_slot(tile, me * clevels + l)
            kx[l, f, :rows] = rolled
            ycorr[f] = merge_slot(ycorr[f], rolled, me * clevels + l)
            hcorr[f * clevels + l] = tile[:H]
            tcorr[f * clevels + l] = tile[rows - H :]

    got_yk = send_y(ycorr, ycorr_in)
    got_xk = send_x(hcorr, tcorr, ncorr, prcorr)
    got_kc = send_corners(ycorr, kcor, kcor_in)

    landed(got_xm)
    landed(got_mc)
    load_halos()
    cut_a = (4 * levels) // 16
    pl.loop(0, cut_a)(member_level)
    landed(got_yk)
    landed(got_xk)
    landed(got_kc)
    load_correction_halos()
    got_shift = []
    cut_b = cut_a
    if square:
        first = []
        for l in range(clevels):
            correction_level(l)
            first.append([send(shift.at[l, k], shift_in.at[k, l, k], near[k]) for k in range(2)])
        for l in range(clevels):
            cut_c = cut_a + (2 * levels * (l + 1)) // 16
            pl.loop(cut_b, cut_c)(member_level)
            cut_b = cut_c
            if l == 0:
                second = [
                    send(shift.at[:, 1 - k], shift_in.at[k, :, 1 - k], near[k]) for k in range(2)
                ]
            landed(first[l])
            got_shift.append([
                send(shift_in.at[k, l, k], shift_in.at[2, l, k], near[1 - k]) for k in range(2)
            ])
    else:
        for l in range(clevels):
            correction_level(l)
            got_shift.append([send(shift.at[l], shift_in.at[k, l], peers[k]) for k in range(n - 1)])
    pl.loop(cut_b, levels)(member_level)

    def add(piece, at):
        for f in range(fields):
            tile = piece[f]
            for m in range(count):
                mf_ref[m, f, at] = mf_ref[m, f, at] + tile

    @pl.loop(0, clevels)
    def _(l):
        add(shift.at[l], me * clevels + l)

    ready = 2 if square else 0
    if square:
        landed(second)
    for k in range(ready):

        @pl.loop(0, clevels)
        def _(l):
            add(shift_in.at[k, l], owners[k] * clevels + l)

    for l in range(clevels):
        landed(got_shift[l])
        for k in range(ready, n - 1):
            add(shift_in.at[k, l], owners[k] * clevels + l)
    for copy in pending:
        copy.wait_send()
    assert len(pending) == copies


def write_kernel(c_ref, m_ref, c_out, m_out, sem):
    group = [
        pltpu.make_async_copy(src, dst, sem.at[k])
        for k, (src, dst) in enumerate(
            [(m_ref, m_out)]
            + [
                (c_ref.at[:, :, c], c_out.at[:, :, :, pl.ds(c * LANES, LANES)])
                for c in range(c_ref.shape[2])
            ]
        )
    ]
    for copy in group:
        copy.start()
    for copy in group:
        copy.wait()


def per_device(control, members, diffusivity, rotation):
    fields, clevels, crows, ccols = control.shape
    count, _, levels, rows, cols = members.shape
    base = count * fields
    tiles = (base + 1) * levels + 1
    wide = ccols // LANES
    n = lax.axis_size("mem")
    ns = 2 if lax.axis_size("gy") > 2 else 1
    copies = 3 * (ns + 2 + 2 * ns) + (8 + 4 * clevels if n == 4 else (1 + clevels) * (n - 1))
    vmem = lambda *shape: pltpu.VMEM(shape, F32)
    height = rows + 2 * H
    scratch = (
        [vmem(fields, clevels, wide, crows + 2 * H, LANES)]
        + [vmem(*a.shape) for a in (members, diffusivity, rotation)]
        + [vmem(fields * clevels, H, ccols)] * 4
        + [vmem(tiles, H, cols)] * 4
        + [vmem(1, crows, LANES), vmem(base + 2, rows, LANES)]
        + [vmem(ns, 1, crows, LANES), vmem(ns, base + 2, rows, LANES)]
        + [vmem(2, 1, H, LANES), vmem(2, base + 2, H, LANES)]
        + [vmem(ns, 2, 1, H, LANES), vmem(ns, 2, base + 2, H, LANES)]
        + [vmem(levels, fields, rows, cols), vmem(n - 1, clevels, fields, rows, cols)]
        + [vmem(clevels, fields, rows, cols)]
        + [vmem(fields * clevels, H, cols)] * 4
        + [vmem(fields, rows, LANES), vmem(ns, fields, rows, LANES)]
        + [vmem(2, fields, H, LANES), vmem(ns, 2, fields, H, LANES)]
        + [vmem(clevels, fields, rows, cols), vmem(n - 1, clevels, fields, rows, cols)]
        + [vmem(count, fields, levels, height, cols), vmem(levels, height, cols), vmem(height, cols)]
        + [vmem(clevels, fields, height, cols), vmem(base + 2, 2 * H, cols), vmem(fields, 2 * H, cols)]
        + [vmem(2, base + 2, height, cols), vmem(2, fields, height, cols), vmem(2, 4, height, cols)]
        + [vmem(count + 1, MSTEPS, fields, height, cols), vmem(height, cols)]
        + [vmem(clevels, fields, rows, cols)]
        + [vmem(2 * H, LANES), vmem(2, crows + 2 * H, LANES)]
        + [vmem(CSTEPS, fields, crows + 2 * H, LANES), vmem(fields, wide, crows + 2 * H, LANES)]
        + [vmem(ccols, ccols // 2)]
        + [pltpu.SemaphoreType.DMA((3 + wide,))] + [pltpu.SemaphoreType.DMA((copies,))] * 2
    )
    space = lambda m, k: [pl.BlockSpec(memory_space=m)] * k
    held = pl.pallas_call(
        functools.partial(fused_kernel, copies),
        in_specs=space(pl.ANY, 4),
        out_specs=space(pltpu.VMEM, 2),
        out_shape=[
            pltpu.VMEM((fields, clevels, wide, crows, LANES), F32), pltpu.VMEM(members.shape, F32)
        ],
        scratch_shapes=scratch,
        compiler_params=pltpu.CompilerParams(
            collective_id=0, has_side_effects=True, vmem_limit_bytes=121 * 2**19
        ),
        name="fused",
    )(control, members, diffusivity, rotation)
    return pl.pallas_call(
        write_kernel,
        in_specs=space(pl.ANY, 2),
        out_specs=space(pl.ANY, 2),
        out_shape=[jax.ShapeDtypeStruct(a.shape, F32) for a in (control, members)],
        scratch_shapes=[pltpu.SemaphoreType.DMA((1 + wide,))],
        compiler_params=pltpu.CompilerParams(vmem_limit_bytes=2**20),
        name="write",
    )(*held)


def solution(mesh):
    in_specs = (
        P(None, "mem", "gx", "gy"),
        P("mem", None, None, "gx", "gy"),
        P(None, "gx", "gy"),
        P("gx", "gy"),
    )
    out_specs = (P(None, "mem", "gx", "gy"), P("mem", None, None, "gx", "gy"))
    return jax.shard_map(
        per_device, mesh=mesh, in_specs=in_specs, out_specs=out_specs, check_vma=False
    )
```

```python
import functools

import jax
import jax.numpy as jnp
from jax import lax
from jax.experimental import pallas as pl
from jax.experimental.pallas import tpu as pltpu
from jax.sharding import PartitionSpec as P

CSTEPS = 4
MSTEPS = 4
H = 4
SLOT = 2 * H
LANES = 128

step_control = 0.15
viscosity = 0.5
step_member = 0.5
F32 = jnp.float32


def lane_ids(rows):
    return lax.broadcasted_iota(jnp.int32, (rows, LANES), 1)


def to_slot(edges, slot):
    shift = H + SLOT * slot
    if not isinstance(slot, int):
        shift = lax.rem(shift, LANES)
    return pltpu.roll(edges, shift, 1)


def merge_slot(packed, rolled, slot):
    ids = lane_ids(rolled.shape[0])
    inside = (ids >= SLOT * slot) & (ids < SLOT * slot + SLOT)
    return jnp.where(inside, rolled, packed)


def put_slot(packed, edges, slot):
    return merge_slot(packed, to_slot(edges, slot), slot)


def side_block(left, right, slot):
    shift = lax.rem(2 * LANES - SLOT * slot - H, LANES)
    after = pltpu.roll(right, shift, 1)
    if left is right:
        return after
    before = pltpu.roll(left, shift, 1)
    return jnp.where(lane_ids(after.shape[0]) < LANES // 2, after, before)


def parts_of(n, clevels):
    if n == 4 and clevels % 2 == 0:
        return [(0, clevels // 2), (clevels // 2, clevels // 2)]
    return [(0, clevels)]


def fused_kernel(
    copies, c_in, m_in, d_in, r_in, cf_ref, mf_ref, c_ref, m_ref, d_ref, r_ref,
    hc, tc, nc, prc, hm, tm, nm, prm, yc, ym, yc_in, ym_in, ccor, mcor, ccor_in, mcor_in,
    sums, sums_in, corr, hcorr, tcorr, ncorr, prcorr, ycorr, ycorr_in, kcor, kcor_in,
    shift, shift_in, mx, dx, rx, kx, ih, kih, strips, kstrips, edge_coef, halos, khalo, part,
    cih, cstrips, chalos, pairs_of, pick,
    load_sem, send_sem, recv_sem,
):
    fields, clevels, wide, cheight, _ = c_ref.shape
    crows, ccols = cheight - 2 * H, wide * LANES
    columns = [slice(c * LANES, (c + 1) * LANES) for c in range(wide)]
    count, _, levels, rows, cols = m_ref.shape
    base = count * fields
    nx, ny, n = lax.axis_size("gx"), lax.axis_size("gy"), lax.axis_size("mem")
    x, y, me = lax.axis_index("gx"), lax.axis_index("gy"), lax.axis_index("mem")
    two = ny > 2
    nsides = 2 if two else 1
    x_next, x_prev = {"gx": lax.rem(x + 1, nx)}, {"gx": lax.rem(x + nx - 1, nx)}
    y_next, y_prev = {"gy": lax.rem(y + 1, ny)}, {"gy": lax.rem(y + ny - 1, ny)}
    peers = [{"mem": lax.rem(me + k, n)} for k in range(1, n)]
    mesh_id = pl.DeviceIdType.MESH
    pending = []

    def send(src, dst, target):
        k = len(pending)
        copy = pltpu.make_async_remote_copy(
            src_ref=src, dst_ref=dst, send_sem=send_sem.at[k], recv_sem=recv_sem.at[k],
            device_id=target, device_id_type=mesh_id,
        )
        copy.start()
        pending.append(copy)
        return copy

    def landed(group):
        for copy in group:
            copy.wait_recv()

    def send_y(src, dst):
        group = [send(src, dst.at[0], y_next)]
        if two:
            group.append(send(src, dst.at[1], y_prev))
        return group

    def send_x(first, last, from_next, from_prev):
        return [send(first, from_next, x_prev), send(last, from_prev, x_next)]

    def send_corners(own, buf, buf_in):
        for g in range(own.shape[0]):
            tile = own[g]
            buf[0, g] = tile[:H]
            buf[1, g] = tile[tile.shape[0] - H :]
        group = []
        for k, across in enumerate([y_next] + ([y_prev] if two else [])):
            group.append(send(buf.at[0], buf_in.at[k, 0], {**x_prev, **across}))
            group.append(send(buf.at[1], buf_in.at[k, 1], {**x_next, **across}))
        return group

    barrier = pltpu.get_barrier_semaphore()
    greeted = [x_next, x_prev, y_next] + ([y_prev] if two else []) + peers
    for across in [y_next] + ([y_prev] if two else []):
        greeted += [{**x_next, **across}, {**x_prev, **across}]
    for target in greeted:
        pl.semaphore_signal(barrier, inc=1, device_id=target, device_id_type=mesh_id)

    loads = [
        pltpu.make_async_copy(src, dst, load_sem.at[k])
        for k, (src, dst) in enumerate(
            [
                (c_in.at[:, :, :, pl.ds(c * LANES, LANES)], c_ref.at[:, :, c, pl.ds(0, crows), :])
                for c in range(wide)
            ]
            + [(m_in, m_ref), (d_in, d_ref), (r_in, r_ref)]
        )
    ]
    for copy in loads:
        copy.start()

    ids = lane_ids(crows)
    yc[...] = jnp.zeros_like(yc)
    ym[...] = jnp.zeros_like(ym)
    ycorr[...] = jnp.zeros_like(ycorr)
    for copy in loads[:wide]:
        copy.wait()

    @pl.loop(0, clevels)
    def _(l):
        for f in range(fields):
            first = c_ref[f, l, 0, :crows]
            last = c_ref[f, l, wide - 1, :crows]
            t = f * clevels + l
            yc[0] = put_slot(yc[0], jnp.where(ids < LANES // 2, first, last), t)
            for c, column in enumerate(columns):
                hc[t, :, column] = c_ref[f, l, c, :H]
                tc[t, :, column] = c_ref[f, l, c, crows - H : crows]

    loads[wide].wait()

    @pl.loop(0, levels)
    def _(l):
        for f in range(fields):
            total = m_ref[0, f, l]
            for m in range(1, count):
                total = total + m_ref[m, f, l]
            sums[l, f] = total

    pl.semaphore_wait(barrier, len(greeted))
    got_yc = send_y(yc, yc_in)
    got_xc = send_x(hc, tc, nc, prc)
    got_cc = send_corners(yc, ccor, ccor_in)
    square = n == 4

    halves = parts_of(n, clevels)
    spans = [pl.ds(first, size) for first, size in halves]

    if square:
        owners = [me + 1 - 2 * lax.rem(me, 2), me + 2 - 4 * (me // 2), 3 - me]
        near = [{"mem": owners[0]}, {"mem": owners[1]}]
        got_far, got_sum = [], []
        for (first, size), span in zip(halves, spans):
            got_far.append([
                send(
                    sums.at[pl.ds(owners[2] * clevels + first, size), k],
                    sums_in.at[2, span, k], near[k],
                )
                for k in range(2)
            ])
        for (first, size), span in zip(halves, spans):
            got_sum.append([
                send(
                    sums.at[pl.ds(owners[k] * clevels + first, size), k],
                    sums_in.at[k, span, k], near[k],
                )
                for k in range(2)
            ])
    else:
        owners = [lax.rem(me + n - 1 - k, n) for k in range(n - 1)]
        got_sum = [[
            send(
                sums.at[pl.ds(lax.rem(me + k, n) * clevels, clevels)],
                sums_in.at[k - 1], peers[k - 1],
            )
            for k in range(1, n)
        ]]
    for copy in loads[wide + 1 :]:
        copy.wait()

    @pl.loop(0, levels)
    def _(l):
        for f in range(fields):
            for m in range(count):
                tile = m_ref[m, f, l]
                g = m * fields + f
                rolled = to_slot(tile, l)
                mx[m, f, l, :rows] = rolled
                ym[g] = merge_slot(ym[g], rolled, l)
                hm[g * levels + l] = tile[:H]
                tm[g * levels + l] = tile[rows - H :]
        tile = d_ref[l]
        rolled = to_slot(tile, l)
        dx[l, :rows] = (0.5 * step_member) * rolled
        ym[base] = merge_slot(ym[base], rolled, l)
        hm[base * levels + l] = tile[:H]
        tm[base * levels + l] = tile[rows - H :]

    tile = r_ref[...]
    rolled = to_slot(tile, 0)
    rx[:rows] = step_member * rolled
    ym[base + 1] = merge_slot(jnp.zeros((rows, LANES), F32), rolled, 0)
    hm[(base + 1) * levels] = tile[:H]
    tm[(base + 1) * levels] = tile[rows - H :]
    got_ym = send_y(ym, ym_in)
    got_mc = send_corners(ym, mcor, mcor_in)
    got_xd, got_xm = [
        send_x(*[ref.at[pl.ds(first, size)] for ref in (hm, tm, nm, prm)])
        for first, size in ((base * levels, levels + 1), (0, base * levels))
    ]
    landed(got_yc)
    landed(got_xc)
    landed(got_cc)

    def pass_sums(h):
        if not square:
            return
        first, size = halves[h]
        for k in range(2):
            landed([got_far[h][k]])

            @pl.loop(first, first + size)
            def _(l):
                part[l, k] = sums[owners[1 - k] * clevels + l, k] + sums_in[2, l, k]

            got_sum[h].append(
                send(part.at[spans[h], k], sums_in.at[1 - k, spans[h], k], near[1 - k])
            )

    pass_sums(0)

    def side_values(body, corners, g):
        out = [
            jnp.concatenate([body[s, g], corners[s, 0, g], corners[s, 1, g]], axis=0)
            for s in range(nsides)
        ]
        return out[0], out[-1]

    height = rows + 2 * H
    side = lax.rem(lane_ids(height), SLOT)

    def load(ref, *at):
        stride = ref.shape[len(at)] // 8
        return jnp.concatenate(
            [ref[(*at, pl.ds(i, 8, stride=stride), slice(None))] for i in range(stride)], axis=0
        )

    def store(ref, value, *at):
        stride, kept = value.shape[0] // 8, ref.shape[len(at)]
        for i in range(stride):
            number = (kept - i + stride - 1) // stride
            ref[(*at, pl.ds(i, number, stride=stride), slice(None))] = value[8 * i : 8 * i + number]

    def up_x(f):
        return jnp.concatenate([f[8:], pltpu.roll(f[:8], 7, 0)], axis=0)

    def low_x(f):
        return jnp.concatenate([pltpu.roll(f[-8:], 1, 0), f[:-8]], axis=0)

    def neighbours(f):
        return pltpu.roll(f, LANES - 1, 1), pltpu.roll(f, 1, 1)

    half_x, half_y = crows // 2, ccols // 2
    cids = lane_ids(cheight)
    cside = lax.rem(cids, SLOT)
    pick[...] = jnp.where(
        lax.broadcasted_iota(jnp.int32, (ccols, half_y), 0) // 2
        == lax.broadcasted_iota(jnp.int32, (ccols, half_y), 1),
        0.25,
        0.0,
    )

    def joined(pair):
        ids = cside[: pair[0].shape[0]]
        return jnp.where(ids == H - 1, pair[0], pair[1])

    def burgers(f, after, before, u, v):
        total = (1.0 - u) * up_x(f) + (1.0 + u) * low_x(f)
        total = total + ((1.0 - v) * after + (1.0 + v) * before)
        diffusion = step_control * viscosity
        return (1.0 - 4.0 * diffusion) * f + diffusion * total

    def load_control_halos():
        cih[...] = jnp.zeros_like(cih)

        @pl.loop(0, clevels)
        def _(l):
            for f in range(fields):
                t = f * clevels + l
                ends = [
                    jnp.concatenate([nc[t, :, column], prc[t, :, column]], axis=0)
                    for column in columns
                ]
                for c in range(wide):
                    c_ref[f, l, c, crows:] = ends[c]
                edge = jnp.where(lane_ids(2 * H) < LANES // 2, ends[0], ends[-1])
                cih[...] = put_slot(cih[...], edge, t)

        own = jnp.concatenate([yc[0], cih[...]], axis=0)
        sides = side_values(yc_in, ccor_in, 0)
        cstrips[0] = jnp.where(cside < H, sides[0], own)
        cstrips[1] = jnp.where(cside < H, own, sides[1])
        first = [load(cstrips, s) for s in range(2)]
        now = [first, [pltpu.roll(f, LANES - SLOT * clevels, 1) for f in first]]
        for step in range(CSTEPS):
            for f in range(fields):
                chalos[step, f] = joined(now[f])
            if step < CSTEPS - 1:
                now = [
                    [burgers(f[s], *neighbours(f[s]), now[0][s], now[1][s]) for s in range(2)]
                    for f in now
                ]

    def control_level(l):
        body = [[load(c_ref, f, l, c) for c in range(wide)] for f in range(fields)]
        for step in range(CSTEPS):
            halo = [
                pltpu.roll(chalos[step, f], LANES - H - SLOT * l, 1) for f in range(fields)
            ]
            new = [[] for _ in range(fields)]
            for c in range(wide):
                sides = []
                for f, field in enumerate(body):
                    right = field[c + 1] if c + 1 < wide else halo[f]
                    left = field[c - 1] if c else halo[f]
                    after = pltpu.roll(jnp.where(cids == 0, right, field[c]), LANES - 1, 1)
                    before = pltpu.roll(jnp.where(cids == LANES - 1, left, field[c]), 1, 1)
                    sides.append((after, before))
                for f, field in enumerate(body):
                    new[f].append(burgers(field[c], *sides[f], body[0][c], body[1][c]))
            body = new
        for f in range(fields):
            for c in range(wide):
                store(cf_ref, body[f][c], f, l, c)
                store(pairs_of, body[f][c] + up_x(body[f][c]), f, c)
        even = [
            jnp.concatenate(
                [pairs_of[f, c, pl.ds(0, half_x, stride=2), :] for c in range(wide)], axis=1
            )
            for f in range(fields)
        ]
        small = jnp.dot(
            jnp.concatenate(even, axis=0), pick[...],
            precision=lax.Precision.HIGHEST, preferred_element_type=F32,
        )
        for f in range(fields):
            corr[l, f] = small[f * half_x : (f + 1) * half_x]

    load_control_halos()
    ids_m = lane_ids(height)

    def move(f, after, before, east, north, south):
        fx = east * (up_x(f) - f)
        return (f + north * (after - f)) + (south * (before - f) + (fx - low_x(fx)))

    def evolve_strips(ref, pairs):
        now = [[[load(ref, s, g) for s in range(2)] for g in pair] for *pair, _ in pairs]
        for step in range(MSTEPS):
            for (*_, at), both in zip(pairs, now):
                for f in range(2):
                    halos[at, step, f] = joined(both[f])
            if step == MSTEPS - 1:
                break
            new = [[[], []] for _ in pairs]
            for s in range(2):
                w = [edge_coef[s, k] for k in range(4)]
                for both, out in zip(now, new):
                    p, q = [move(f[s], *neighbours(f[s]), *w[:3]) for f in both]
                    out[0].append(p - w[3] * both[1][s])
                    out[1].append(q + w[3] * both[0][s])
            now = new

    def pack_strips(own, halo, body, corners, g, out, at):
        own = jnp.concatenate([own, halo], axis=0)
        sides = side_values(body, corners, g)
        out[0, at] = jnp.where(side < H, sides[0], own)
        out[1, at] = jnp.where(side < H, own, sides[1])

    def load_halo(g, l):
        t = g * levels + l
        halo = to_slot(jnp.concatenate([nm[t], prm[t]], axis=0), l)
        ih[g] = merge_slot(ih[g], halo, l)
        return halo

    def load_coefficients():
        ih[...] = jnp.zeros_like(ih)

        @pl.loop(0, levels)
        def _(l):
            dx[l, rows:] = (0.5 * step_member) * load_halo(base, l)

        rx[rows:] = step_member * load_halo(base + 1, 0)
        for g in (base, base + 1):
            pack_strips(ym[g], ih[g], ym_in, mcor_in, g, strips, g)
        kappa = [(0.5 * step_member) * load(strips, s, base) for s in range(2)]
        khalo[...] = joined(kappa)
        for s in range(2):
            f = kappa[s]
            after, before = neighbours(f)
            edge_coef[s, 0] = f + up_x(f)
            edge_coef[s, 1] = f + after
            edge_coef[s, 2] = f + before
            spin = jnp.where(ids_m < SLOT, step_member * load(strips, s, base + 1), 0.0)
            width = SLOT
            while width < LANES:
                spin = spin + pltpu.roll(spin, width, 1)
                width *= 2
            edge_coef[s, 3] = spin

    def load_halos():
        @pl.loop(0, levels)
        def _(l):
            for g in range(base):
                mx[g // fields, g % fields, l, rows:] = load_halo(g, l)

        for g in range(base):
            pack_strips(ym[g], ih[g], ym_in, mcor_in, g, strips, g)
        evolve_strips(strips, [(m * fields, m * fields + 1, m) for m in range(count)])

    def evolve(levels_of):
        state, setting = [], []
        for l, work in levels_of:
            first = SLOT * l + H
            is_first, is_last = ids_m == first, ids_m == first - 1

            def beside(f, halo, is_first=is_first, is_last=is_last):
                after = pltpu.roll(jnp.where(is_first, halo, f), LANES - 1, 1)
                before = pltpu.roll(jnp.where(is_last, halo, f), 1, 1)
                return after, before

            kappa = load(dx, l)
            after, before = beside(kappa, khalo[...])
            weights = kappa + up_x(kappa), kappa + after, kappa + before
            spin = pltpu.roll(load(rx), SLOT * l, 1)
            for p, q, m in work:
                state.append((p, q))
                setting.append((m, beside, weights, spin, first))
        for step in range(MSTEPS):
            new = []
            for (p, q), (m, beside, weights, spin, _) in zip(state, setting):
                moved = [
                    move(f, *beside(f, halos[m, step, k]), *weights) for k, f in enumerate((p, q))
                ]
                new.append((moved[0] - spin * q, moved[1] + spin * p))
            state = new
        return [
            [pltpu.roll(f, LANES - first, 1) for f in pair]
            for pair, (*_, first) in zip(state, setting)
        ]

    def member_level(l):
        work = [(*[load(mx, m, f, l) for f in range(fields)], m) for m in range(count)]
        for m, pair in enumerate(evolve([(l, work)])):
            for f in range(fields):
                store(mf_ref, pair[f], m, f, l)

    def load_correction_halos(h):
        kih[...] = jnp.zeros_like(kih)
        first, size = halves[h]

        @pl.loop(first, first + size)
        def _(l):
            for f in range(fields):
                t = l * fields + f
                halo = to_slot(jnp.concatenate([ncorr[t], prcorr[t]], axis=0), me * clevels + l)
                kih[f] = merge_slot(kih[f], halo, me * clevels + l)
                kx[l, f, rows:] = halo

        for f in range(fields):
            pack_strips(ycorr[h, f], kih[f], ycorr_in.at[h], kcor_in.at[h], f, kstrips, f)
        evolve_strips(kstrips, [(0, 1, count)])

    def correction_levels(first, size):
        at = [first + i for i in range(size)]
        work = [
            (me * clevels + l, [(*[load(kx, l, f) for f in range(fields)], count)]) for l in at
        ]
        for l, pair in zip(at, evolve(work)):
            for f in range(fields):
                store(shift, pair[f], l, f)

    def correct(h):
        landed(got_sum[h])
        first, size = halves[h]

        @pl.loop(first, first + size)
        def _(l):
            for f in range(fields):
                total = sums[me * clevels + l, f]
                for k in range(2 if square else n - 1):
                    total = total + sums_in[k, l, f]
                tile = corr[l, f] - total * (1.0 / (count * n))
                rolled = to_slot(tile, me * clevels + l)
                kx[l, f, :rows] = rolled
                ycorr[h, f] = merge_slot(ycorr[h, f], rolled, me * clevels + l)
                hcorr[l * fields + f] = tile[:H]
                tcorr[l * fields + f] = tile[rows - H :]

        span = pl.ds(first * fields, size * fields)
        group = send_y(ycorr.at[h], ycorr_in.at[h])
        group += send_x(*[ref.at[span] for ref in (hcorr, tcorr, ncorr, prcorr)])
        return group + send_corners(ycorr.at[h], kcor.at[h], kcor_in.at[h])

    ahead, got_shift, rest = [], [], []

    def shift_levels(h):
        landed(got_k[h])
        load_correction_halos(h)
        first, size = halves[h]
        correction_levels(first, size)
        for l in range(first, first + size):
            if square:
                ahead.append([
                    send(shift.at[l, k], shift_in.at[k, l, k], near[k]) for k in range(2)
                ])
            else:
                got_shift.append([
                    send(shift.at[l], shift_in.at[k, l], peers[k]) for k in range(n - 1)
                ])

    def shift_rest(h):
        for k in range(2 if square else 0):
            rest.append(
                send(shift.at[spans[h], 1 - k], shift_in.at[k, spans[h], 1 - k], near[k])
            )

    def forward(l):
        if square:
            landed(ahead[l])
            got_shift.append([
                send(shift_in.at[k, l, k], shift_in.at[2, l, k], near[1 - k]) for k in range(2)
            ])

    done = 0

    def member_levels(sixteenths):
        nonlocal done
        stop = min(done + max(1, sixteenths * levels // 16), levels)
        pl.loop(done, stop)(member_level)
        done = stop

    def control_part(h):
        pl.loop(halves[h][0], halves[h][0] + halves[h][1])(control_level)

    control_part(0)
    if len(halves) > 1:
        pass_sums(1)
    for group in (got_ym, got_xd, got_mc):
        landed(group)
    load_coefficients()
    got_k = [correct(0)]
    for h in range(1, len(halves)):
        control_part(h)
        got_k.append(correct(h))
    shift_levels(0)
    shift_rest(0)
    landed(got_xm)
    load_halos()
    member_levels(2)
    for h in range(1, len(halves)):
        shift_levels(h)
        shift_rest(h)
    for l, gap in enumerate((3,1,4,1)):
        if gap:
            member_levels(gap)
        forward(l)
    pl.loop(done, levels)(member_level)

    def add(piece, at):
        for f in range(fields):
            tile = piece[f]
            for m in range(count):
                mf_ref[m, f, at] = mf_ref[m, f, at] + tile

    @pl.loop(0, clevels)
    def _(l):
        add(shift.at[l], me * clevels + l)

    ready = 2 if square else 0
    if square:
        landed(rest)
    for k in range(ready):

        @pl.loop(0, clevels)
        def _(l):
            add(shift_in.at[k, l], owners[k] * clevels + l)

    for l in range(clevels):
        landed(got_shift[l])
        for k in range(ready, n - 1):
            add(shift_in.at[k, l], owners[k] * clevels + l)
    for copy in pending:
        copy.wait_send()
    assert len(pending) == copies


def write_kernel(c_ref, m_ref, c_out, m_out, sem):
    group = [
        pltpu.make_async_copy(src, dst, sem.at[k])
        for k, (src, dst) in enumerate(
            [(m_ref, m_out)]
            + [
                (c_ref.at[:, :, c], c_out.at[:, :, :, pl.ds(c * LANES, LANES)])
                for c in range(c_ref.shape[2])
            ]
        )
    ]
    for copy in group:
        copy.start()
    for copy in group:
        copy.wait()


def per_device(control, members, diffusivity, rotation):
    fields, clevels, crows, ccols = control.shape
    count, _, levels, rows, cols = members.shape
    base = count * fields
    tiles = (base + 1) * levels + 1
    wide = ccols // LANES
    n = lax.axis_size("mem")
    ns = 2 if lax.axis_size("gy") > 2 else 1
    many = len(parts_of(n, clevels))
    copies = (2 + many) * (ns + 2 + 2 * ns) + 2
    copies += 8 * many + 4 * clevels if n == 4 else (1 + clevels) * (n - 1)
    vmem = lambda *shape: pltpu.VMEM(shape, F32)
    height = rows + 2 * H
    scratch = (
        [vmem(fields, clevels, wide, crows + 2 * H, LANES)]
        + [vmem(*a.shape) for a in (members, diffusivity, rotation)]
        + [vmem(fields * clevels, H, ccols)] * 4
        + [vmem(tiles, H, cols)] * 4
        + [vmem(1, crows, LANES), vmem(base + 2, rows, LANES)]
        + [vmem(ns, 1, crows, LANES), vmem(ns, base + 2, rows, LANES)]
        + [vmem(2, 1, H, LANES), vmem(2, base + 2, H, LANES)]
        + [vmem(ns, 2, 1, H, LANES), vmem(ns, 2, base + 2, H, LANES)]
        + [vmem(levels, fields, rows, cols), vmem(n - 1, clevels, fields, rows, cols)]
        + [vmem(clevels, fields, rows, cols)]
        + [vmem(fields * clevels, H, cols)] * 4
        + [vmem(many, fields, rows, LANES), vmem(many, ns, fields, rows, LANES)]
        + [vmem(many, 2, fields, H, LANES), vmem(many, ns, 2, fields, H, LANES)]
        + [vmem(clevels, fields, rows, cols), vmem(n - 1, clevels, fields, rows, cols)]
        + [vmem(count, fields, levels, height, cols), vmem(levels, height, cols), vmem(height, cols)]
        + [vmem(clevels, fields, height, cols), vmem(base + 2, 2 * H, cols), vmem(fields, 2 * H, cols)]
        + [vmem(2, base + 2, height, cols), vmem(2, fields, height, cols), vmem(2, 4, height, cols)]
        + [vmem(count + 1, MSTEPS, fields, height, cols), vmem(height, cols)]
        + [vmem(clevels, fields, rows, cols)]
        + [vmem(2 * H, LANES), vmem(2, crows + 2 * H, LANES)]
        + [vmem(CSTEPS, fields, crows + 2 * H, LANES), vmem(fields, wide, crows + 2 * H, LANES)]
        + [vmem(ccols, ccols // 2)]
        + [pltpu.SemaphoreType.DMA((3 + wide,))] + [pltpu.SemaphoreType.DMA((copies,))] * 2
    )
    space = lambda m, k: [pl.BlockSpec(memory_space=m)] * k
    held = pl.pallas_call(
        functools.partial(fused_kernel, copies),
        in_specs=space(pl.ANY, 4),
        out_specs=space(pltpu.VMEM, 2),
        out_shape=[
            pltpu.VMEM((fields, clevels, wide, crows, LANES), F32), pltpu.VMEM(members.shape, F32)
        ],
        scratch_shapes=scratch,
        compiler_params=pltpu.CompilerParams(
            collective_id=0, has_side_effects=True, vmem_limit_bytes=121 * 2**19
        ),
        name="fused",
    )(control, members, diffusivity, rotation)
    return pl.pallas_call(
        write_kernel,
        in_specs=space(pl.ANY, 2),
        out_specs=space(pl.ANY, 2),
        out_shape=[jax.ShapeDtypeStruct(a.shape, F32) for a in (control, members)],
        scratch_shapes=[pltpu.SemaphoreType.DMA((1 + wide,))],
        compiler_params=pltpu.CompilerParams(vmem_limit_bytes=2**20),
        name="write",
    )(*held)


def solution(mesh):
    in_specs = (
        P(None, "mem", "gx", "gy"),
        P("mem", None, None, "gx", "gy"),
        P(None, "gx", "gy"),
        P("gx", "gy"),
    )
    out_specs = (P(None, "mem", "gx", "gy"), P("mem", None, None, "gx", "gy"))
    return jax.shard_map(
        per_device, mesh=mesh, in_specs=in_specs, out_specs=out_specs, check_vma=False
    )
```

```python
import functools

import jax
import jax.numpy as jnp
from jax import lax
from jax.experimental import pallas as pl
from jax.experimental.pallas import tpu as pltpu
from jax.sharding import PartitionSpec as P

CSTEPS = 4
MSTEPS = 4
H = 4
SLOT = 2 * H
LANES = 128

step_control = 0.15
viscosity = 0.5
step_member = 0.5
F32 = jnp.float32


def lane_ids(rows):
    return lax.broadcasted_iota(jnp.int32, (rows, LANES), 1)


def to_slot(edges, slot):
    shift = H + SLOT * slot
    if not isinstance(slot, int):
        shift = lax.rem(shift, LANES)
    return pltpu.roll(edges, shift, 1)


def merge_slot(packed, rolled, slot):
    ids = lane_ids(rolled.shape[0])
    inside = (ids >= SLOT * slot) & (ids < SLOT * slot + SLOT)
    return jnp.where(inside, rolled, packed)


def put_slot(packed, edges, slot):
    return merge_slot(packed, to_slot(edges, slot), slot)


def side_block(left, right, slot):
    shift = lax.rem(2 * LANES - SLOT * slot - H, LANES)
    after = pltpu.roll(right, shift, 1)
    if left is right:
        return after
    before = pltpu.roll(left, shift, 1)
    return jnp.where(lane_ids(after.shape[0]) < LANES // 2, after, before)


def parts_of(n, clevels):
    if n == 4 and clevels % 2 == 0:
        return [(0, clevels // 2), (clevels // 2, clevels // 2)]
    return [(0, clevels)]


def fused_kernel(
    copies, c_in, m_in, d_in, r_in, cf_ref, mf_ref, c_ref, m_ref, d_ref, r_ref,
    hc, tc, nc, prc, hm, tm, nm, prm, yc, ym, yc_in, ym_in, ccor, mcor, ccor_in, mcor_in,
    sums, sums_in, corr, hcorr, tcorr, ncorr, prcorr, ycorr, ycorr_in, kcor, kcor_in,
    shift, shift_in, mx, dx, rx, kx, ih, kih, strips, kstrips, edge_coef, halos, khalo, part,
    cih, cstrips, chalos, pairs_of, pick,
    load_sem, send_sem, recv_sem,
):
    fields, clevels, wide, cheight, _ = c_ref.shape
    crows, ccols = cheight - 2 * H, wide * LANES
    columns = [slice(c * LANES, (c + 1) * LANES) for c in range(wide)]
    count, _, levels, rows, cols = m_ref.shape
    base = count * fields
    nx, ny, n = lax.axis_size("gx"), lax.axis_size("gy"), lax.axis_size("mem")
    x, y, me = lax.axis_index("gx"), lax.axis_index("gy"), lax.axis_index("mem")
    two = ny > 2
    nsides = 2 if two else 1
    x_next, x_prev = {"gx": lax.rem(x + 1, nx)}, {"gx": lax.rem(x + nx - 1, nx)}
    y_next, y_prev = {"gy": lax.rem(y + 1, ny)}, {"gy": lax.rem(y + ny - 1, ny)}
    peers = [{"mem": lax.rem(me + k, n)} for k in range(1, n)]
    mesh_id = pl.DeviceIdType.MESH
    pending = []

    def send(src, dst, target):
        k = len(pending)
        copy = pltpu.make_async_remote_copy(
            src_ref=src, dst_ref=dst, send_sem=send_sem.at[k], recv_sem=recv_sem.at[k],
            device_id=target, device_id_type=mesh_id,
        )
        copy.start()
        pending.append(copy)
        return copy

    def landed(group):
        for copy in group:
            copy.wait_recv()

    def send_y(src, dst):
        group = [send(src, dst.at[0], y_next)]
        if two:
            group.append(send(src, dst.at[1], y_prev))
        return group

    def send_x(first, last, from_next, from_prev):
        return [send(first, from_next, x_prev), send(last, from_prev, x_next)]

    def send_corners(own, buf, buf_in):
        for g in range(own.shape[0]):
            tile = own[g]
            buf[0, g] = tile[:H]
            buf[1, g] = tile[tile.shape[0] - H :]
        group = []
        for k, across in enumerate([y_next] + ([y_prev] if two else [])):
            group.append(send(buf.at[0], buf_in.at[k, 0], {**x_prev, **across}))
            group.append(send(buf.at[1], buf_in.at[k, 1], {**x_next, **across}))
        return group

    barrier = pltpu.get_barrier_semaphore()
    greeted = [x_next, x_prev, y_next] + ([y_prev] if two else []) + peers
    for across in [y_next] + ([y_prev] if two else []):
        greeted += [{**x_next, **across}, {**x_prev, **across}]
    for target in greeted:
        pl.semaphore_signal(barrier, inc=1, device_id=target, device_id_type=mesh_id)

    loads = [
        pltpu.make_async_copy(src, dst, load_sem.at[k])
        for k, (src, dst) in enumerate(
            [
                (c_in.at[:, :, :, pl.ds(c * LANES, LANES)], c_ref.at[:, :, c, pl.ds(0, crows), :])
                for c in range(wide)
            ]
            + [(m_in, m_ref), (d_in, d_ref), (r_in, r_ref)]
        )
    ]
    for copy in loads:
        copy.start()

    ids = lane_ids(crows)
    yc[...] = jnp.zeros_like(yc)
    ym[...] = jnp.zeros_like(ym)
    ycorr[...] = jnp.zeros_like(ycorr)
    for copy in loads[:wide]:
        copy.wait()

    @pl.loop(0, clevels)
    def _(l):
        for f in range(fields):
            first = c_ref[f, l, 0, :crows]
            last = c_ref[f, l, wide - 1, :crows]
            t = f * clevels + l
            yc[0] = put_slot(yc[0], jnp.where(ids < LANES // 2, first, last), t)
            for c, column in enumerate(columns):
                hc[t, :, column] = c_ref[f, l, c, :H]
                tc[t, :, column] = c_ref[f, l, c, crows - H : crows]

    pl.semaphore_wait(barrier, len(greeted))
    got_yc = send_y(yc, yc_in)
    got_xc = send_x(hc, tc, nc, prc)
    got_cc = send_corners(yc, ccor, ccor_in)
    square = n == 4

    loads[wide].wait()

    @pl.loop(0, levels)
    def _(l):
        for f in range(fields):
            total = m_ref[0, f, l]
            for m in range(1, count):
                total = total + m_ref[m, f, l]
            sums[l, f] = total

    halves = parts_of(n, clevels)
    spans = [pl.ds(first, size) for first, size in halves]

    if square:
        owners = [me + 1 - 2 * lax.rem(me, 2), me + 2 - 4 * (me // 2), 3 - me]
        near = [{"mem": owners[0]}, {"mem": owners[1]}]
        got_far, got_sum = [], []
        for (first, size), span in zip(halves, spans):
            got_far.append([
                send(
                    sums.at[pl.ds(owners[2] * clevels + first, size), k],
                    sums_in.at[2, span, k], near[k],
                )
                for k in range(2)
            ])
        for (first, size), span in zip(halves, spans):
            got_sum.append([
                send(
                    sums.at[pl.ds(owners[k] * clevels + first, size), k],
                    sums_in.at[k, span, k], near[k],
                )
                for k in range(2)
            ])
    else:
        owners = [lax.rem(me + n - 1 - k, n) for k in range(n - 1)]
        got_sum = [[
            send(
                sums.at[pl.ds(lax.rem(me + k, n) * clevels, clevels)],
                sums_in.at[k - 1], peers[k - 1],
            )
            for k in range(1, n)
        ]]
    for copy in loads[wide + 1 :]:
        copy.wait()

    @pl.loop(0, levels)
    def _(l):
        for f in range(fields):
            for m in range(count):
                tile = m_ref[m, f, l]
                g = m * fields + f
                rolled = to_slot(tile, l)
                mx[m, f, l, :rows] = rolled
                ym[g] = merge_slot(ym[g], rolled, l)
                hm[g * levels + l] = tile[:H]
                tm[g * levels + l] = tile[rows - H :]
        tile = d_ref[l]
        rolled = to_slot(tile, l)
        dx[l, :rows] = (0.5 * step_member) * rolled
        ym[base] = merge_slot(ym[base], rolled, l)
        hm[base * levels + l] = tile[:H]
        tm[base * levels + l] = tile[rows - H :]

    tile = r_ref[...]
    rolled = to_slot(tile, 0)
    rx[:rows] = step_member * rolled
    ym[base + 1] = merge_slot(jnp.zeros((rows, LANES), F32), rolled, 0)
    hm[(base + 1) * levels] = tile[:H]
    tm[(base + 1) * levels] = tile[rows - H :]
    got_ym = send_y(ym, ym_in)
    got_mc = send_corners(ym, mcor, mcor_in)
    got_xd, got_xm = [
        send_x(*[ref.at[pl.ds(first, size)] for ref in (hm, tm, nm, prm)])
        for first, size in ((base * levels, levels + 1), (0, base * levels))
    ]
    landed(got_yc)
    landed(got_xc)
    landed(got_cc)

    def pass_sums(h):
        if not square:
            return
        first, size = halves[h]
        for k in range(2):
            landed([got_far[h][k]])

            @pl.loop(first, first + size)
            def _(l):
                part[l, k] = sums[owners[1 - k] * clevels + l, k] + sums_in[2, l, k]

            got_sum[h].append(
                send(part.at[spans[h], k], sums_in.at[1 - k, spans[h], k], near[1 - k])
            )

    pass_sums(0)

    def side_values(body, corners, g):
        out = [
            jnp.concatenate([body[s, g], corners[s, 0, g], corners[s, 1, g]], axis=0)
            for s in range(nsides)
        ]
        return out[0], out[-1]

    height = rows + 2 * H
    side = lax.rem(lane_ids(height), SLOT)

    def load(ref, *at):
        stride = ref.shape[len(at)] // 8
        return jnp.concatenate(
            [ref[(*at, pl.ds(i, 8, stride=stride), slice(None))] for i in range(stride)], axis=0
        )

    def store(ref, value, *at):
        stride, kept = value.shape[0] // 8, ref.shape[len(at)]
        for i in range(stride):
            number = (kept - i + stride - 1) // stride
            ref[(*at, pl.ds(i, number, stride=stride), slice(None))] = value[8 * i : 8 * i + number]

    def up_x(f):
        return jnp.concatenate([f[8:], pltpu.roll(f[:8], 7, 0)], axis=0)

    def low_x(f):
        return jnp.concatenate([pltpu.roll(f[-8:], 1, 0), f[:-8]], axis=0)

    def neighbours(f):
        return pltpu.roll(f, LANES - 1, 1), pltpu.roll(f, 1, 1)

    half_x, half_y = crows // 2, ccols // 2
    cids = lane_ids(cheight)
    cside = lax.rem(cids, SLOT)
    pick[...] = jnp.where(
        lax.broadcasted_iota(jnp.int32, (ccols, half_y), 0) // 2
        == lax.broadcasted_iota(jnp.int32, (ccols, half_y), 1),
        0.25,
        0.0,
    )

    def joined(pair):
        ids = cside[: pair[0].shape[0]]
        return jnp.where(ids == H - 1, pair[0], pair[1])

    def burgers(f, after, before, u, v):
        total = (1.0 - u) * up_x(f) + (1.0 + u) * low_x(f)
        total = total + ((1.0 - v) * after + (1.0 + v) * before)
        diffusion = step_control * viscosity
        return (1.0 - 4.0 * diffusion) * f + diffusion * total

    def load_control_halos():
        cih[...] = jnp.zeros_like(cih)

        @pl.loop(0, clevels)
        def _(l):
            for f in range(fields):
                t = f * clevels + l
                ends = [
                    jnp.concatenate([nc[t, :, column], prc[t, :, column]], axis=0)
                    for column in columns
                ]
                for c in range(wide):
                    c_ref[f, l, c, crows:] = ends[c]
                edge = jnp.where(lane_ids(2 * H) < LANES // 2, ends[0], ends[-1])
                cih[...] = put_slot(cih[...], edge, t)

        own = jnp.concatenate([yc[0], cih[...]], axis=0)
        sides = side_values(yc_in, ccor_in, 0)
        cstrips[0] = jnp.where(cside < H, sides[0], own)
        cstrips[1] = jnp.where(cside < H, own, sides[1])
        first = [load(cstrips, s) for s in range(2)]
        now = [first, [pltpu.roll(f, LANES - SLOT * clevels, 1) for f in first]]
        for step in range(CSTEPS):
            for f in range(fields):
                chalos[step, f] = joined(now[f])
            if step < CSTEPS - 1:
                now = [
                    [burgers(f[s], *neighbours(f[s]), now[0][s], now[1][s]) for s in range(2)]
                    for f in now
                ]

    def control_level(l):
        body = [[load(c_ref, f, l, c) for c in range(wide)] for f in range(fields)]
        for step in range(CSTEPS):
            halo = [
                pltpu.roll(chalos[step, f], LANES - H - SLOT * l, 1) for f in range(fields)
            ]
            new = [[] for _ in range(fields)]
            for c in range(wide):
                sides = []
                for f, field in enumerate(body):
                    right = field[c + 1] if c + 1 < wide else halo[f]
                    left = field[c - 1] if c else halo[f]
                    after = pltpu.roll(jnp.where(cids == 0, right, field[c]), LANES - 1, 1)
                    before = pltpu.roll(jnp.where(cids == LANES - 1, left, field[c]), 1, 1)
                    sides.append((after, before))
                for f, field in enumerate(body):
                    new[f].append(burgers(field[c], *sides[f], body[0][c], body[1][c]))
            body = new
        for f in range(fields):
            for c in range(wide):
                store(cf_ref, body[f][c], f, l, c)
                store(pairs_of, body[f][c] + up_x(body[f][c]), f, c)
        even = [
            jnp.concatenate(
                [pairs_of[f, c, pl.ds(0, half_x, stride=2), :] for c in range(wide)], axis=1
            )
            for f in range(fields)
        ]
        small = jnp.dot(
            jnp.concatenate(even, axis=0), pick[...],
            precision=lax.Precision.HIGHEST, preferred_element_type=F32,
        )
        for f in range(fields):
            corr[l, f] = small[f * half_x : (f + 1) * half_x]

    load_control_halos()
    ids_m = lane_ids(height)

    def move(f, after, before, east, north, south):
        fx = east * (up_x(f) - f)
        return (f + north * (after - f)) + (south * (before - f) + (fx - low_x(fx)))

    def evolve_strips(ref, pairs):
        now = [[[load(ref, s, g) for s in range(2)] for g in pair] for *pair, _ in pairs]
        for step in range(MSTEPS):
            for (*_, at), both in zip(pairs, now):
                for f in range(2):
                    halos[at, step, f] = joined(both[f])
            if step == MSTEPS - 1:
                break
            new = [[[], []] for _ in pairs]
            for s in range(2):
                w = [edge_coef[s, k] for k in range(4)]
                for both, out in zip(now, new):
                    p, q = [move(f[s], *neighbours(f[s]), *w[:3]) for f in both]
                    out[0].append(p - w[3] * both[1][s])
                    out[1].append(q + w[3] * both[0][s])
            now = new

    def pack_strips(own, halo, body, corners, g, out, at):
        own = jnp.concatenate([own, halo], axis=0)
        sides = side_values(body, corners, g)
        out[0, at] = jnp.where(side < H, sides[0], own)
        out[1, at] = jnp.where(side < H, own, sides[1])

    def load_halo(g, l):
        t = g * levels + l
        halo = to_slot(jnp.concatenate([nm[t], prm[t]], axis=0), l)
        ih[g] = merge_slot(ih[g], halo, l)
        return halo

    def load_coefficients():
        ih[...] = jnp.zeros_like(ih)

        @pl.loop(0, levels)
        def _(l):
            dx[l, rows:] = (0.5 * step_member) * load_halo(base, l)

        rx[rows:] = step_member * load_halo(base + 1, 0)
        for g in (base, base + 1):
            pack_strips(ym[g], ih[g], ym_in, mcor_in, g, strips, g)
        kappa = [(0.5 * step_member) * load(strips, s, base) for s in range(2)]
        khalo[...] = joined(kappa)
        for s in range(2):
            f = kappa[s]
            after, before = neighbours(f)
            edge_coef[s, 0] = f + up_x(f)
            edge_coef[s, 1] = f + after
            edge_coef[s, 2] = f + before
            spin = jnp.where(ids_m < SLOT, step_member * load(strips, s, base + 1), 0.0)
            width = SLOT
            while width < LANES:
                spin = spin + pltpu.roll(spin, width, 1)
                width *= 2
            edge_coef[s, 3] = spin

    def load_halos():
        @pl.loop(0, levels)
        def _(l):
            for g in range(base):
                mx[g // fields, g % fields, l, rows:] = load_halo(g, l)

        for g in range(base):
            pack_strips(ym[g], ih[g], ym_in, mcor_in, g, strips, g)
        evolve_strips(strips, [(m * fields, m * fields + 1, m) for m in range(count)])

    def evolve(levels_of):
        state, setting = [], []
        for l, work in levels_of:
            first = SLOT * l + H
            is_first, is_last = ids_m == first, ids_m == first - 1

            def beside(f, halo, is_first=is_first, is_last=is_last):
                after = pltpu.roll(jnp.where(is_first, halo, f), LANES - 1, 1)
                before = pltpu.roll(jnp.where(is_last, halo, f), 1, 1)
                return after, before

            kappa = load(dx, l)
            after, before = beside(kappa, khalo[...])
            weights = kappa + up_x(kappa), kappa + after, kappa + before
            spin = pltpu.roll(load(rx), SLOT * l, 1)
            for p, q, m in work:
                state.append((p, q))
                setting.append((m, beside, weights, spin, first))
        for step in range(MSTEPS):
            new = []
            for (p, q), (m, beside, weights, spin, _) in zip(state, setting):
                moved = [
                    move(f, *beside(f, halos[m, step, k]), *weights) for k, f in enumerate((p, q))
                ]
                new.append((moved[0] - spin * q, moved[1] + spin * p))
            state = new
        return [
            [pltpu.roll(f, LANES - first, 1) for f in pair]
            for pair, (*_, first) in zip(state, setting)
        ]

    def member_level(l):
        work = [(*[load(mx, m, f, l) for f in range(fields)], m) for m in range(count)]
        for m, pair in enumerate(evolve([(l, work)])):
            for f in range(fields):
                store(mf_ref, pair[f], m, f, l)

    def load_correction_halos(h):
        kih[...] = jnp.zeros_like(kih)
        first, size = halves[h]

        @pl.loop(first, first + size)
        def _(l):
            for f in range(fields):
                t = l * fields + f
                halo = to_slot(jnp.concatenate([ncorr[t], prcorr[t]], axis=0), me * clevels + l)
                kih[f] = merge_slot(kih[f], halo, me * clevels + l)
                kx[l, f, rows:] = halo

        for f in range(fields):
            pack_strips(ycorr[h, f], kih[f], ycorr_in.at[h], kcor_in.at[h], f, kstrips, f)
        evolve_strips(kstrips, [(0, 1, count)])

    def correction_levels(first, size):
        at = [first + i for i in range(size)]
        work = [
            (me * clevels + l, [(*[load(kx, l, f) for f in range(fields)], count)]) for l in at
        ]
        for l, pair in zip(at, evolve(work)):
            for f in range(fields):
                store(shift, pair[f], l, f)

    def correct(h):
        landed(got_sum[h])
        first, size = halves[h]

        @pl.loop(first, first + size)
        def _(l):
            for f in range(fields):
                total = sums[me * clevels + l, f]
                for k in range(2 if square else n - 1):
                    total = total + sums_in[k, l, f]
                tile = corr[l, f] - total * (1.0 / (count * n))
                rolled = to_slot(tile, me * clevels + l)
                kx[l, f, :rows] = rolled
                ycorr[h, f] = merge_slot(ycorr[h, f], rolled, me * clevels + l)
                hcorr[l * fields + f] = tile[:H]
                tcorr[l * fields + f] = tile[rows - H :]

        span = pl.ds(first * fields, size * fields)
        group = send_y(ycorr.at[h], ycorr_in.at[h])
        group += send_x(*[ref.at[span] for ref in (hcorr, tcorr, ncorr, prcorr)])
        return group + send_corners(ycorr.at[h], kcor.at[h], kcor_in.at[h])

    ahead, got_shift, rest = [], [], []

    def shift_levels(h):
        landed(got_k[h])
        load_correction_halos(h)
        first, size = halves[h]
        correction_levels(first, size)
        for l in range(first, first + size):
            if square:
                ahead.append([
                    send(shift.at[l, k], shift_in.at[k, l, k], near[k]) for k in range(2)
                ])
            else:
                got_shift.append([
                    send(shift.at[l], shift_in.at[k, l], peers[k]) for k in range(n - 1)
                ])

    def shift_rest(h):
        for k in range(2 if square else 0):
            rest.append(
                send(shift.at[spans[h], 1 - k], shift_in.at[k, spans[h], 1 - k], near[k])
            )

    def forward(l):
        if square:
            landed(ahead[l])
            got_shift.append([
                send(shift_in.at[k, l, k], shift_in.at[2, l, k], near[1 - k]) for k in range(2)
            ])

    done = 0

    def member_levels(sixteenths):
        nonlocal done
        stop = min(done + max(1, sixteenths * levels // 16), levels)
        pl.loop(done, stop)(member_level)
        done = stop

    def control_part(h):
        pl.loop(halves[h][0], halves[h][0] + halves[h][1])(control_level)

    control_part(0)
    if len(halves) > 1:
        pass_sums(1)
    for group in (got_ym, got_xd, got_mc):
        landed(group)
    load_coefficients()
    got_k = [correct(0)]
    for h in range(1, len(halves)):
        control_part(h)
        got_k.append(correct(h))
    shift_levels(0)
    shift_rest(0)
    landed(got_xm)
    load_halos()
    member_levels(2)
    for h in range(1, len(halves)):
        shift_levels(h)
        shift_rest(h)
    for l in range(clevels):
        member_levels(1 if l % halves[0][1] else 4 if l else 3)
        forward(l)
    pl.loop(done, levels)(member_level)

    def add(piece, at):
        for f in range(fields):
            tile = piece[f]
            for m in range(count):
                mf_ref[m, f, at] = mf_ref[m, f, at] + tile

    @pl.loop(0, clevels)
    def _(l):
        add(shift.at[l], me * clevels + l)

    ready = 2 if square else 0
    if square:
        landed(rest)
    for k in range(ready):

        @pl.loop(0, clevels)
        def _(l):
            add(shift_in.at[k, l], owners[k] * clevels + l)

    for l in range(clevels):
        landed(got_shift[l])
        for k in range(ready, n - 1):
            add(shift_in.at[k, l], owners[k] * clevels + l)
    for copy in pending:
        copy.wait_send()
    assert len(pending) == copies


def write_kernel(c_ref, m_ref, c_out, m_out, sem):
    group = [
        pltpu.make_async_copy(src, dst, sem.at[k])
        for k, (src, dst) in enumerate(
            [(m_ref, m_out)]
            + [
                (c_ref.at[:, :, c], c_out.at[:, :, :, pl.ds(c * LANES, LANES)])
                for c in range(c_ref.shape[2])
            ]
        )
    ]
    for copy in group:
        copy.start()
    for copy in group:
        copy.wait()


def per_device(control, members, diffusivity, rotation):
    fields, clevels, crows, ccols = control.shape
    count, _, levels, rows, cols = members.shape
    base = count * fields
    tiles = (base + 1) * levels + 1
    wide = ccols // LANES
    n = lax.axis_size("mem")
    ns = 2 if lax.axis_size("gy") > 2 else 1
    many = len(parts_of(n, clevels))
    copies = (2 + many) * (ns + 2 + 2 * ns) + 2
    copies += 8 * many + 4 * clevels if n == 4 else (1 + clevels) * (n - 1)
    vmem = lambda *shape: pltpu.VMEM(shape, F32)
    height = rows + 2 * H
    scratch = (
        [vmem(fields, clevels, wide, crows + 2 * H, LANES)]
        + [vmem(*a.shape) for a in (members, diffusivity, rotation)]
        + [vmem(fields * clevels, H, ccols)] * 4
        + [vmem(tiles, H, cols)] * 4
        + [vmem(1, crows, LANES), vmem(base + 2, rows, LANES)]
        + [vmem(ns, 1, crows, LANES), vmem(ns, base + 2, rows, LANES)]
        + [vmem(2, 1, H, LANES), vmem(2, base + 2, H, LANES)]
        + [vmem(ns, 2, 1, H, LANES), vmem(ns, 2, base + 2, H, LANES)]
        + [vmem(levels, fields, rows, cols), vmem(n - 1, clevels, fields, rows, cols)]
        + [vmem(clevels, fields, rows, cols)]
        + [vmem(fields * clevels, H, cols)] * 4
        + [vmem(many, fields, rows, LANES), vmem(many, ns, fields, rows, LANES)]
        + [vmem(many, 2, fields, H, LANES), vmem(many, ns, 2, fields, H, LANES)]
        + [vmem(clevels, fields, rows, cols), vmem(n - 1, clevels, fields, rows, cols)]
        + [vmem(count, fields, levels, height, cols), vmem(levels, height, cols), vmem(height, cols)]
        + [vmem(clevels, fields, height, cols), vmem(base + 2, 2 * H, cols), vmem(fields, 2 * H, cols)]
        + [vmem(2, base + 2, height, cols), vmem(2, fields, height, cols), vmem(2, 4, height, cols)]
        + [vmem(count + 1, MSTEPS, fields, height, cols), vmem(height, cols)]
        + [vmem(clevels, fields, rows, cols)]
        + [vmem(2 * H, LANES), vmem(2, crows + 2 * H, LANES)]
        + [vmem(CSTEPS, fields, crows + 2 * H, LANES), vmem(fields, wide, crows + 2 * H, LANES)]
        + [vmem(ccols, ccols // 2)]
        + [pltpu.SemaphoreType.DMA((3 + wide,))] + [pltpu.SemaphoreType.DMA((copies,))] * 2
    )
    space = lambda m, k: [pl.BlockSpec(memory_space=m)] * k
    held = pl.pallas_call(
        functools.partial(fused_kernel, copies),
        in_specs=space(pl.ANY, 4),
        out_specs=space(pltpu.VMEM, 2),
        out_shape=[
            pltpu.VMEM((fields, clevels, wide, crows, LANES), F32), pltpu.VMEM(members.shape, F32)
        ],
        scratch_shapes=scratch,
        compiler_params=pltpu.CompilerParams(
            collective_id=0, has_side_effects=True, vmem_limit_bytes=121 * 2**19
        ),
        name="fused",
    )(control, members, diffusivity, rotation)
    return pl.pallas_call(
        write_kernel,
        in_specs=space(pl.ANY, 2),
        out_specs=space(pl.ANY, 2),
        out_shape=[jax.ShapeDtypeStruct(a.shape, F32) for a in (control, members)],
        scratch_shapes=[pltpu.SemaphoreType.DMA((1 + wide,))],
        compiler_params=pltpu.CompilerParams(vmem_limit_bytes=2**20),
        name="write",
    )(*held)


def solution(mesh):
    in_specs = (
        P(None, "mem", "gx", "gy"),
        P("mem", None, None, "gx", "gy"),
        P(None, "gx", "gy"),
        P("gx", "gy"),
    )
    out_specs = (P(None, "mem", "gx", "gy"), P("mem", None, None, "gx", "gy"))
    return jax.shard_map(
        per_device, mesh=mesh, in_specs=in_specs, out_specs=out_specs, check_vma=False
    )
```

```python
import functools

import jax
import jax.numpy as jnp
from jax import lax
from jax.experimental import pallas as pl
from jax.experimental.pallas import tpu as pltpu
from jax.sharding import PartitionSpec as P

CSTEPS = 4
MSTEPS = 4
H = 4
SLOT = 2 * H
LANES = 128

step_control = 0.15
viscosity = 0.5
step_member = 0.5
F32 = jnp.float32


def lane_ids(rows):
    return lax.broadcasted_iota(jnp.int32, (rows, LANES), 1)


def to_slot(edges, slot):
    shift = H + SLOT * slot
    if not isinstance(slot, int):
        shift = lax.rem(shift, LANES)
    return pltpu.roll(edges, shift, 1)


def merge_slot(packed, rolled, slot):
    ids = lane_ids(rolled.shape[0])
    inside = (ids >= SLOT * slot) & (ids < SLOT * slot + SLOT)
    return jnp.where(inside, rolled, packed)


def put_slot(packed, edges, slot):
    return merge_slot(packed, to_slot(edges, slot), slot)


def side_block(left, right, slot):
    shift = lax.rem(2 * LANES - SLOT * slot - H, LANES)
    after = pltpu.roll(right, shift, 1)
    if left is right:
        return after
    before = pltpu.roll(left, shift, 1)
    return jnp.where(lane_ids(after.shape[0]) < LANES // 2, after, before)


def parts_of(n, clevels):
    if n == 4 and clevels % 2 == 0:
        return [(0, clevels // 2), (clevels // 2, clevels // 2)]
    return [(0, clevels)]


def fused_kernel(
    copies, c_in, m_in, d_in, r_in, cf_ref, mf_ref, c_ref, m_ref, d_ref, r_ref,
    hc, tc, nc, prc, hm, tm, nm, prm, yc, ym, yc_in, ym_in, ccor, mcor, ccor_in, mcor_in,
    sums, sums_in, corr, hcorr, tcorr, ncorr, prcorr, ycorr, ycorr_in, kcor, kcor_in,
    shift, shift_in, mx, dx, rx, kx, ih, kih, strips, kstrips, edge_coef, halos, khalo, part,
    cih, cstrips, chalos, pairs_of, pick,
    load_sem, send_sem, recv_sem,
):
    fields, clevels, wide, cheight, _ = c_ref.shape
    crows, ccols = cheight - 2 * H, wide * LANES
    columns = [slice(c * LANES, (c + 1) * LANES) for c in range(wide)]
    count, _, levels, rows, cols = m_ref.shape
    base = count * fields
    nx, ny, n = lax.axis_size("gx"), lax.axis_size("gy"), lax.axis_size("mem")
    x, y, me = lax.axis_index("gx"), lax.axis_index("gy"), lax.axis_index("mem")
    two = ny > 2
    nsides = 2 if two else 1
    x_next, x_prev = {"gx": lax.rem(x + 1, nx)}, {"gx": lax.rem(x + nx - 1, nx)}
    y_next, y_prev = {"gy": lax.rem(y + 1, ny)}, {"gy": lax.rem(y + ny - 1, ny)}
    peers = [{"mem": lax.rem(me + k, n)} for k in range(1, n)]
    mesh_id = pl.DeviceIdType.MESH
    pending = []

    def send(src, dst, target):
        k = len(pending)
        copy = pltpu.make_async_remote_copy(
            src_ref=src, dst_ref=dst, send_sem=send_sem.at[k], recv_sem=recv_sem.at[k],
            device_id=target, device_id_type=mesh_id,
        )
        copy.start()
        pending.append(copy)
        return copy

    def landed(group):
        for copy in group:
            copy.wait_recv()

    def send_y(src, dst):
        group = [send(src, dst.at[0], y_next)]
        if two:
            group.append(send(src, dst.at[1], y_prev))
        return group

    def send_x(first, last, from_next, from_prev):
        return [send(first, from_next, x_prev), send(last, from_prev, x_next)]

    def send_corners(own, buf, buf_in):
        for g in range(own.shape[0]):
            tile = own[g]
            buf[0, g] = tile[:H]
            buf[1, g] = tile[tile.shape[0] - H :]
        group = []
        for k, across in enumerate([y_next] + ([y_prev] if two else [])):
            group.append(send(buf.at[0], buf_in.at[k, 0], {**x_prev, **across}))
            group.append(send(buf.at[1], buf_in.at[k, 1], {**x_next, **across}))
        return group

    barrier = pltpu.get_barrier_semaphore()
    greeted = [x_next, x_prev, y_next] + ([y_prev] if two else []) + peers
    for across in [y_next] + ([y_prev] if two else []):
        greeted += [{**x_next, **across}, {**x_prev, **across}]
    for target in greeted:
        pl.semaphore_signal(barrier, inc=1, device_id=target, device_id_type=mesh_id)

    loads = [
        pltpu.make_async_copy(src, dst, load_sem.at[k])
        for k, (src, dst) in enumerate(
            [
                (c_in.at[:, :, :, pl.ds(c * LANES, LANES)], c_ref.at[:, :, c, pl.ds(0, crows), :])
                for c in range(wide)
            ]
            + [(d_in, d_ref), (r_in, r_ref)]
            + [(m_in.at[m, f], m_ref.at[m, f]) for m in range(count) for f in range(fields)]
        )
    ]
    for copy in loads:
        copy.start()

    ids = lane_ids(crows)
    yc[...] = jnp.zeros_like(yc)
    ym[...] = jnp.zeros_like(ym)
    ycorr[...] = jnp.zeros_like(ycorr)
    for copy in loads[:wide]:
        copy.wait()

    @pl.loop(0, clevels)
    def _(l):
        for f in range(fields):
            first = c_ref[f, l, 0, :crows]
            last = c_ref[f, l, wide - 1, :crows]
            t = f * clevels + l
            yc[0] = put_slot(yc[0], jnp.where(ids < LANES // 2, first, last), t)
            for c, column in enumerate(columns):
                hc[t, :, column] = c_ref[f, l, c, :H]
                tc[t, :, column] = c_ref[f, l, c, crows - H : crows]

    pl.semaphore_wait(barrier, len(greeted))
    got_yc = send_y(yc, yc_in)
    got_xc = send_x(hc, tc, nc, prc)
    got_cc = send_corners(yc, ccor, ccor_in)
    square = n == 4

    for copy in loads[wide + 2 :]:
        copy.wait()

    @pl.loop(0, levels)
    def _(l):
        for f in range(fields):
            total = m_ref[0, f, l]
            for m in range(1, count):
                total = total + m_ref[m, f, l]
            sums[l, f] = total

    halves = parts_of(n, clevels)
    spans = [pl.ds(first, size) for first, size in halves]

    if square:
        owners = [me + 1 - 2 * lax.rem(me, 2), me + 2 - 4 * (me // 2), 3 - me]
        near = [{"mem": owners[0]}, {"mem": owners[1]}]
        got_far, got_sum = [], []
        for (first, size), span in zip(halves, spans):
            got_far.append([
                send(
                    sums.at[pl.ds(owners[2] * clevels + first, size), k],
                    sums_in.at[2, span, k], near[k],
                )
                for k in range(2)
            ])
        for (first, size), span in zip(halves, spans):
            got_sum.append([
                send(
                    sums.at[pl.ds(owners[k] * clevels + first, size), k],
                    sums_in.at[k, span, k], near[k],
                )
                for k in range(2)
            ])
    else:
        owners = [lax.rem(me + n - 1 - k, n) for k in range(n - 1)]
        got_sum = [[
            send(
                sums.at[pl.ds(lax.rem(me + k, n) * clevels, clevels)],
                sums_in.at[k - 1], peers[k - 1],
            )
            for k in range(1, n)
        ]]
    for copy in loads[wide : wide + 2]:
        copy.wait()

    @pl.loop(0, levels)
    def _(l):
        for f in range(fields):
            for m in range(count):
                tile = m_ref[m, f, l]
                g = m * fields + f
                rolled = to_slot(tile, l)
                mx[m, f, l, :rows] = rolled
                ym[g] = merge_slot(ym[g], rolled, l)
                hm[g * levels + l] = tile[:H]
                tm[g * levels + l] = tile[rows - H :]
        tile = d_ref[l]
        rolled = to_slot(tile, l)
        dx[l, :rows] = (0.5 * step_member) * rolled
        ym[base] = merge_slot(ym[base], rolled, l)
        hm[base * levels + l] = tile[:H]
        tm[base * levels + l] = tile[rows - H :]

    tile = r_ref[...]
    rolled = to_slot(tile, 0)
    rx[:rows] = step_member * rolled
    ym[base + 1] = merge_slot(jnp.zeros((rows, LANES), F32), rolled, 0)
    hm[(base + 1) * levels] = tile[:H]
    tm[(base + 1) * levels] = tile[rows - H :]
    got_ym = send_y(ym, ym_in)
    got_mc = send_corners(ym, mcor, mcor_in)
    got_xd, got_xm = [
        send_x(*[ref.at[pl.ds(first, size)] for ref in (hm, tm, nm, prm)])
        for first, size in ((base * levels, levels + 1), (0, base * levels))
    ]
    landed(got_yc)
    landed(got_xc)
    landed(got_cc)

    def pass_sums(h):
        if not square:
            return
        first, size = halves[h]
        for k in range(2):
            landed([got_far[h][k]])

            @pl.loop(first, first + size)
            def _(l):
                part[l, k] = sums[owners[1 - k] * clevels + l, k] + sums_in[2, l, k]

            got_sum[h].append(
                send(part.at[spans[h], k], sums_in.at[1 - k, spans[h], k], near[1 - k])
            )

    pass_sums(0)

    def side_values(body, corners, g):
        out = [
            jnp.concatenate([body[s, g], corners[s, 0, g], corners[s, 1, g]], axis=0)
            for s in range(nsides)
        ]
        return out[0], out[-1]

    height = rows + 2 * H
    side = lax.rem(lane_ids(height), SLOT)

    def load(ref, *at):
        stride = ref.shape[len(at)] // 8
        return jnp.concatenate(
            [ref[(*at, pl.ds(i, 8, stride=stride), slice(None))] for i in range(stride)], axis=0
        )

    def store(ref, value, *at):
        stride, kept = value.shape[0] // 8, ref.shape[len(at)]
        for i in range(stride):
            number = (kept - i + stride - 1) // stride
            ref[(*at, pl.ds(i, number, stride=stride), slice(None))] = value[8 * i : 8 * i + number]

    def up_x(f):
        return jnp.concatenate([f[8:], pltpu.roll(f[:8], 7, 0)], axis=0)

    def low_x(f):
        return jnp.concatenate([pltpu.roll(f[-8:], 1, 0), f[:-8]], axis=0)

    def neighbours(f):
        return pltpu.roll(f, LANES - 1, 1), pltpu.roll(f, 1, 1)

    half_x, half_y = crows // 2, ccols // 2
    cids = lane_ids(cheight)
    cside = lax.rem(cids, SLOT)
    pick[...] = jnp.where(
        lax.broadcasted_iota(jnp.int32, (ccols, half_y), 0) // 2
        == lax.broadcasted_iota(jnp.int32, (ccols, half_y), 1),
        0.25,
        0.0,
    )

    def joined(pair):
        ids = cside[: pair[0].shape[0]]
        return jnp.where(ids == H - 1, pair[0], pair[1])

    def burgers(f, after, before, u, v):
        total = (1.0 - u) * up_x(f) + (1.0 + u) * low_x(f)
        total = total + ((1.0 - v) * after + (1.0 + v) * before)
        diffusion = step_control * viscosity
        return (1.0 - 4.0 * diffusion) * f + diffusion * total

    def load_control_halos():
        cih[...] = jnp.zeros_like(cih)

        @pl.loop(0, clevels)
        def _(l):
            for f in range(fields):
                t = f * clevels + l
                ends = [
                    jnp.concatenate([nc[t, :, column], prc[t, :, column]], axis=0)
                    for column in columns
                ]
                for c in range(wide):
                    c_ref[f, l, c, crows:] = ends[c]
                edge = jnp.where(lane_ids(2 * H) < LANES // 2, ends[0], ends[-1])
                cih[...] = put_slot(cih[...], edge, t)

        own = jnp.concatenate([yc[0], cih[...]], axis=0)
        sides = side_values(yc_in, ccor_in, 0)
        cstrips[0] = jnp.where(cside < H, sides[0], own)
        cstrips[1] = jnp.where(cside < H, own, sides[1])
        first = [load(cstrips, s) for s in range(2)]
        now = [first, [pltpu.roll(f, LANES - SLOT * clevels, 1) for f in first]]
        for step in range(CSTEPS):
            for f in range(fields):
                chalos[step, f] = joined(now[f])
            if step < CSTEPS - 1:
                now = [
                    [burgers(f[s], *neighbours(f[s]), now[0][s], now[1][s]) for s in range(2)]
                    for f in now
                ]

    def control_level(l):
        body = [[load(c_ref, f, l, c) for c in range(wide)] for f in range(fields)]
        for step in range(CSTEPS):
            halo = [
                pltpu.roll(chalos[step, f], LANES - H - SLOT * l, 1) for f in range(fields)
            ]
            new = [[] for _ in range(fields)]
            for c in range(wide):
                sides = []
                for f, field in enumerate(body):
                    right = field[c + 1] if c + 1 < wide else halo[f]
                    left = field[c - 1] if c else halo[f]
                    after = pltpu.roll(jnp.where(cids == 0, right, field[c]), LANES - 1, 1)
                    before = pltpu.roll(jnp.where(cids == LANES - 1, left, field[c]), 1, 1)
                    sides.append((after, before))
                for f, field in enumerate(body):
                    new[f].append(burgers(field[c], *sides[f], body[0][c], body[1][c]))
            body = new
        for f in range(fields):
            for c in range(wide):
                store(cf_ref, body[f][c], f, l, c)
                store(pairs_of, body[f][c] + up_x(body[f][c]), f, c)
        even = [
            jnp.concatenate(
                [pairs_of[f, c, pl.ds(0, half_x, stride=2), :] for c in range(wide)], axis=1
            )
            for f in range(fields)
        ]
        small = jnp.dot(
            jnp.concatenate(even, axis=0), pick[...],
            precision=lax.Precision.HIGHEST, preferred_element_type=F32,
        )
        for f in range(fields):
            corr[l, f] = small[f * half_x : (f + 1) * half_x]

    load_control_halos()
    ids_m = lane_ids(height)

    def move(f, after, before, east, north, south):
        fx = east * (up_x(f) - f)
        return (f + north * (after - f)) + (south * (before - f) + (fx - low_x(fx)))

    def evolve_strips(ref, pairs):
        now = [[[load(ref, s, g) for s in range(2)] for g in pair] for *pair, _ in pairs]
        for step in range(MSTEPS):
            for (*_, at), both in zip(pairs, now):
                for f in range(2):
                    halos[at, step, f] = joined(both[f])
            if step == MSTEPS - 1:
                break
            new = [[[], []] for _ in pairs]
            for s in range(2):
                w = [edge_coef[s, k] for k in range(4)]
                for both, out in zip(now, new):
                    p, q = [move(f[s], *neighbours(f[s]), *w[:3]) for f in both]
                    out[0].append(p - w[3] * both[1][s])
                    out[1].append(q + w[3] * both[0][s])
            now = new

    def pack_strips(own, halo, body, corners, g, out, at):
        own = jnp.concatenate([own, halo], axis=0)
        sides = side_values(body, corners, g)
        out[0, at] = jnp.where(side < H, sides[0], own)
        out[1, at] = jnp.where(side < H, own, sides[1])

    def load_halo(g, l):
        t = g * levels + l
        halo = to_slot(jnp.concatenate([nm[t], prm[t]], axis=0), l)
        ih[g] = merge_slot(ih[g], halo, l)
        return halo

    def load_coefficients():
        ih[...] = jnp.zeros_like(ih)

        @pl.loop(0, levels)
        def _(l):
            dx[l, rows:] = (0.5 * step_member) * load_halo(base, l)

        rx[rows:] = step_member * load_halo(base + 1, 0)
        for g in (base, base + 1):
            pack_strips(ym[g], ih[g], ym_in, mcor_in, g, strips, g)
        kappa = [(0.5 * step_member) * load(strips, s, base) for s in range(2)]
        khalo[...] = joined(kappa)
        for s in range(2):
            f = kappa[s]
            after, before = neighbours(f)
            edge_coef[s, 0] = f + up_x(f)
            edge_coef[s, 1] = f + after
            edge_coef[s, 2] = f + before
            spin = jnp.where(ids_m < SLOT, step_member * load(strips, s, base + 1), 0.0)
            width = SLOT
            while width < LANES:
                spin = spin + pltpu.roll(spin, width, 1)
                width *= 2
            edge_coef[s, 3] = spin

    def load_halos():
        @pl.loop(0, levels)
        def _(l):
            for g in range(base):
                mx[g // fields, g % fields, l, rows:] = load_halo(g, l)

        for g in range(base):
            pack_strips(ym[g], ih[g], ym_in, mcor_in, g, strips, g)
        evolve_strips(strips, [(m * fields, m * fields + 1, m) for m in range(count)])

    def evolve(levels_of):
        state, setting = [], []
        for l, work in levels_of:
            first = SLOT * l + H
            is_first, is_last = ids_m == first, ids_m == first - 1

            def beside(f, halo, is_first=is_first, is_last=is_last):
                after = pltpu.roll(jnp.where(is_first, halo, f), LANES - 1, 1)
                before = pltpu.roll(jnp.where(is_last, halo, f), 1, 1)
                return after, before

            kappa = load(dx, l)
            after, before = beside(kappa, khalo[...])
            weights = kappa + up_x(kappa), kappa + after, kappa + before
            spin = pltpu.roll(load(rx), SLOT * l, 1)
            for p, q, m in work:
                state.append((p, q))
                setting.append((m, beside, weights, spin, first))
        for step in range(MSTEPS):
            new = []
            for (p, q), (m, beside, weights, spin, _) in zip(state, setting):
                moved = [
                    move(f, *beside(f, halos[m, step, k]), *weights) for k, f in enumerate((p, q))
                ]
                new.append((moved[0] - spin * q, moved[1] + spin * p))
            state = new
        return [
            [pltpu.roll(f, LANES - first, 1) for f in pair]
            for pair, (*_, first) in zip(state, setting)
        ]

    def member_level(l):
        work = [(*[load(mx, m, f, l) for f in range(fields)], m) for m in range(count)]
        for m, pair in enumerate(evolve([(l, work)])):
            for f in range(fields):
                store(mf_ref, pair[f], m, f, l)

    def load_correction_halos(h):
        kih[...] = jnp.zeros_like(kih)
        first, size = halves[h]

        @pl.loop(first, first + size)
        def _(l):
            for f in range(fields):
                t = l * fields + f
                halo = to_slot(jnp.concatenate([ncorr[t], prcorr[t]], axis=0), me * clevels + l)
                kih[f] = merge_slot(kih[f], halo, me * clevels + l)
                kx[l, f, rows:] = halo

        for f in range(fields):
            pack_strips(ycorr[h, f], kih[f], ycorr_in.at[h], kcor_in.at[h], f, kstrips, f)
        evolve_strips(kstrips, [(0, 1, count)])

    def correction_levels(first, size):
        at = [first + i for i in range(size)]
        work = [
            (me * clevels + l, [(*[load(kx, l, f) for f in range(fields)], count)]) for l in at
        ]
        for l, pair in zip(at, evolve(work)):
            for f in range(fields):
                store(shift, pair[f], l, f)

    def correct(h):
        landed(got_sum[h])
        first, size = halves[h]

        @pl.loop(first, first + size)
        def _(l):
            for f in range(fields):
                total = sums[me * clevels + l, f]
                for k in range(2 if square else n - 1):
                    total = total + sums_in[k, l, f]
                tile = corr[l, f] - total * (1.0 / (count * n))
                rolled = to_slot(tile, me * clevels + l)
                kx[l, f, :rows] = rolled
                ycorr[h, f] = merge_slot(ycorr[h, f], rolled, me * clevels + l)
                hcorr[l * fields + f] = tile[:H]
                tcorr[l * fields + f] = tile[rows - H :]

        span = pl.ds(first * fields, size * fields)
        group = send_y(ycorr.at[h], ycorr_in.at[h])
        group += send_x(*[ref.at[span] for ref in (hcorr, tcorr, ncorr, prcorr)])
        return group + send_corners(ycorr.at[h], kcor.at[h], kcor_in.at[h])

    ahead, got_shift, rest = [], [], []

    def shift_levels(h):
        landed(got_k[h])
        load_correction_halos(h)
        first, size = halves[h]
        correction_levels(first, size)
        for l in range(first, first + size):
            if square:
                ahead.append([
                    send(shift.at[l, k], shift_in.at[k, l, k], near[k]) for k in range(2)
                ])
            else:
                got_shift.append([
                    send(shift.at[l], shift_in.at[k, l], peers[k]) for k in range(n - 1)
                ])

    def shift_rest(h):
        for k in range(2 if square else 0):
            rest.append(
                send(shift.at[spans[h], 1 - k], shift_in.at[k, spans[h], 1 - k], near[k])
            )

    def forward(l):
        if square:
            landed(ahead[l])
            got_shift.append([
                send(shift_in.at[k, l, k], shift_in.at[2, l, k], near[1 - k]) for k in range(2)
            ])

    done = 0

    def member_levels(sixteenths):
        nonlocal done
        stop = min(done + max(1, sixteenths * levels // 16), levels)
        pl.loop(done, stop)(member_level)
        done = stop

    def control_part(h):
        pl.loop(halves[h][0], halves[h][0] + halves[h][1])(control_level)

    control_part(0)
    if len(halves) > 1:
        pass_sums(1)
    for group in (got_ym, got_xd, got_mc):
        landed(group)
    load_coefficients()
    got_k = [correct(0)]
    for h in range(1, len(halves)):
        control_part(h)
        got_k.append(correct(h))
    shift_levels(0)
    shift_rest(0)
    landed(got_xm)
    load_halos()
    member_levels(2)
    for h in range(1, len(halves)):
        shift_levels(h)
        shift_rest(h)
    for l in range(clevels):
        member_levels(1 if l % halves[0][1] else 4 if l else 3)
        forward(l)
    pl.loop(done, levels)(member_level)

    def add(piece, at):
        for f in range(fields):
            tile = piece[f]
            for m in range(count):
                mf_ref[m, f, at] = mf_ref[m, f, at] + tile

    @pl.loop(0, clevels)
    def _(l):
        add(shift.at[l], me * clevels + l)

    ready = 2 if square else 0
    if square:
        landed(rest)
    for k in range(ready):

        @pl.loop(0, clevels)
        def _(l):
            add(shift_in.at[k, l], owners[k] * clevels + l)

    for l in range(clevels):
        landed(got_shift[l])
        for k in range(ready, n - 1):
            add(shift_in.at[k, l], owners[k] * clevels + l)
    for copy in pending:
        copy.wait_send()
    assert len(pending) == copies


def write_kernel(c_ref, m_ref, c_out, m_out, sem):
    group = [
        pltpu.make_async_copy(src, dst, sem.at[k])
        for k, (src, dst) in enumerate(
            [(m_ref, m_out)]
            + [
                (c_ref.at[:, :, c], c_out.at[:, :, :, pl.ds(c * LANES, LANES)])
                for c in range(c_ref.shape[2])
            ]
        )
    ]
    for copy in group:
        copy.start()
    for copy in group:
        copy.wait()


def per_device(control, members, diffusivity, rotation):
    fields, clevels, crows, ccols = control.shape
    count, _, levels, rows, cols = members.shape
    base = count * fields
    tiles = (base + 1) * levels + 1
    wide = ccols // LANES
    n = lax.axis_size("mem")
    ns = 2 if lax.axis_size("gy") > 2 else 1
    many = len(parts_of(n, clevels))
    copies = (2 + many) * (ns + 2 + 2 * ns) + 2
    copies += 8 * many + 4 * clevels if n == 4 else (1 + clevels) * (n - 1)
    vmem = lambda *shape: pltpu.VMEM(shape, F32)
    height = rows + 2 * H
    scratch = (
        [vmem(fields, clevels, wide, crows + 2 * H, LANES)]
        + [vmem(*a.shape) for a in (members, diffusivity, rotation)]
        + [vmem(fields * clevels, H, ccols)] * 4
        + [vmem(tiles, H, cols)] * 4
        + [vmem(1, crows, LANES), vmem(base + 2, rows, LANES)]
        + [vmem(ns, 1, crows, LANES), vmem(ns, base + 2, rows, LANES)]
        + [vmem(2, 1, H, LANES), vmem(2, base + 2, H, LANES)]
        + [vmem(ns, 2, 1, H, LANES), vmem(ns, 2, base + 2, H, LANES)]
        + [vmem(levels, fields, rows, cols), vmem(n - 1, clevels, fields, rows, cols)]
        + [vmem(clevels, fields, rows, cols)]
        + [vmem(fields * clevels, H, cols)] * 4
        + [vmem(many, fields, rows, LANES), vmem(many, ns, fields, rows, LANES)]
        + [vmem(many, 2, fields, H, LANES), vmem(many, ns, 2, fields, H, LANES)]
        + [vmem(clevels, fields, rows, cols), vmem(n - 1, clevels, fields, rows, cols)]
        + [vmem(count, fields, levels, height, cols), vmem(levels, height, cols), vmem(height, cols)]
        + [vmem(clevels, fields, height, cols), vmem(base + 2, 2 * H, cols), vmem(fields, 2 * H, cols)]
        + [vmem(2, base + 2, height, cols), vmem(2, fields, height, cols), vmem(2, 4, height, cols)]
        + [vmem(count + 1, MSTEPS, fields, height, cols), vmem(height, cols)]
        + [vmem(clevels, fields, rows, cols)]
        + [vmem(2 * H, LANES), vmem(2, crows + 2 * H, LANES)]
        + [vmem(CSTEPS, fields, crows + 2 * H, LANES), vmem(fields, wide, crows + 2 * H, LANES)]
        + [vmem(ccols, ccols // 2)]
        + [pltpu.SemaphoreType.DMA((2 + base + wide,))] + [pltpu.SemaphoreType.DMA((copies,))] * 2
    )
    space = lambda m, k: [pl.BlockSpec(memory_space=m)] * k
    held = pl.pallas_call(
        functools.partial(fused_kernel, copies),
        in_specs=space(pl.ANY, 4),
        out_specs=space(pltpu.VMEM, 2),
        out_shape=[
            pltpu.VMEM((fields, clevels, wide, crows, LANES), F32), pltpu.VMEM(members.shape, F32)
        ],
        scratch_shapes=scratch,
        compiler_params=pltpu.CompilerParams(
            collective_id=0, has_side_effects=True, vmem_limit_bytes=121 * 2**19
        ),
        name="fused",
    )(control, members, diffusivity, rotation)
    return pl.pallas_call(
        write_kernel,
        in_specs=space(pl.ANY, 2),
        out_specs=space(pl.ANY, 2),
        out_shape=[jax.ShapeDtypeStruct(a.shape, F32) for a in (control, members)],
        scratch_shapes=[pltpu.SemaphoreType.DMA((1 + wide,))],
        compiler_params=pltpu.CompilerParams(vmem_limit_bytes=2**20),
        name="write",
    )(*held)


def solution(mesh):
    in_specs = (
        P(None, "mem", "gx", "gy"),
        P("mem", None, None, "gx", "gy"),
        P(None, "gx", "gy"),
        P("gx", "gy"),
    )
    out_specs = (P(None, "mem", "gx", "gy"), P("mem", None, None, "gx", "gy"))
    return jax.shard_map(
        per_device, mesh=mesh, in_specs=in_specs, out_specs=out_specs, check_vma=False
    )
```
